32 devices in a mesh: seq: 16 (over z, x, core), fsdp: 2 (over y).
Axes of the slice: x: 2, y: 2, z: 4, core: 2. Of those that a mesh axis runs over, the one named last changes fastest.
Arguments:
- hidden: bfloat16 [2, 4096, 1024], P('fsdp', 'seq')
- w_qkv: bfloat16 [1024, 3072], P('fsdp')
- cond_vec: bfloat16 [1024], replicated, may hold values from -6 to 6
- head_w: bfloat16 [1024], replicated, may hold values from -0.1875 to 0.1875
- blocks: int32 [2, 64, 5], P('fsdp', 'seq'), may hold values from 0 to 63, as said below
- counts: int32 [2, 64], P('fsdp', 'seq'), may hold values from 1 to 4, 128 in all within a row
- time_idx: int32 [2, 4096], P('fsdp', 'seq'), may hold values from 0 to 999
- cond_mask: int32 [2, 4096], P('fsdp', 'seq'), may hold values 0 or 1
- noise: float32 [2, 4096], P('fsdp', 'seq'), may hold values from -6 to 6
Outputs:
- d_hidden: bfloat16 [2, 4096, 1024], P('fsdp', 'seq')
- grad_qkv: float32 [1024, 3072], P('fsdp')
The draws below stay inside these ranges and needn't reach their ends.
Inputs may be any that keep to these rules, and one draw needn't show every extreme that they name: Each list holds 5 distinct blocks of its own sequence: slot 0 is the query block itself, slot 1 a block exactly 4 blocks before or after it around the cycle of 64 blocks, and the other slots blocks within 4 of it around that cycle. Each sequence's counts sum to 128.
All inputs are finite; a program needn't handle non-finite values. No bound on the sum of `counts` or of `cond_mask` on one device may be relied on, other than what follows from the above.
Results may differ from the reference program's by a relative error of at most 0.014.
Values may be sent and summed in bfloat16 or wider, within the bound.
A program may use at most 128 MiB of HBM per device.

```python
import math
import jax
import jax.numpy as jnp
import numpy as np
from jax import lax

D = 1024
H = 16
HD = 64
BLK = 64
REACH = 4
NB = 5
STEPS = 1000
SEQS = 2
LEN = 4096
NBLK = 64


def draw_hidden(key, part):
    first = jax.random.fold_in(key, 0)
    base = jax.random.normal(first, (SEQS, LEN, D), jnp.float32)
    return base.astype(jnp.bfloat16)


def draw_w_qkv(key, part):
    first = jax.random.fold_in(key, 0)
    base = jax.random.normal(first, (D, 3 * D), jnp.float32) * D ** (-0.5)
    return base.astype(jnp.bfloat16)


def draw_blocks(key, part):
    first, second = jax.random.split(jax.random.fold_in(key, 7))
    total_rows = SEQS * NBLK
    side = jax.random.randint(first, (total_rows, 1), 0, 2, jnp.int32) * 2 - 1
    offsets_all = jnp.concatenate([jnp.arange(-REACH, 0, dtype=jnp.int32), jnp.arange(1, REACH + 1, dtype=jnp.int32)])
    ranking = jax.random.randint(second, (total_rows, 2 * REACH), 0, 65536, jnp.int32) * (2 * REACH)
    ranking = ranking + jnp.arange(2 * REACH, dtype=jnp.int32)[None, :]
    ranking = jnp.where(offsets_all[None, :] == side * REACH, -1, ranking)
    unused, picks = lax.top_k(ranking, NB - 2)
    others = offsets_all[picks]
    offsets = jnp.concatenate([jnp.zeros((total_rows, 1), jnp.int32), side * REACH, others], axis=1)
    own = jnp.tile(jnp.arange(NBLK, dtype=jnp.int32), SEQS)[:, None]
    return jnp.remainder(own + offsets, NBLK).astype(jnp.int32).reshape(SEQS, NBLK, NB)


def place_ends(entries, rng, smallest, largest):
    shape = entries.shape
    spot = [jax.random.randint(jax.random.fold_in(rng, axis), (), 0, shape[axis]) for axis in range(len(shape))]
    entries = entries.at[tuple(spot)].set(smallest)
    longest = shape.index(max(shape))
    spot[longest] = (spot[longest] + 1) % shape[longest]
    return entries.at[tuple(spot)].set(largest)


def level_of(stream_key, dims, cuts, smallest, largest):
    gain, own = 1.0, jax.random.fold_in(stream_key, 6)
    for axis_at, parts in cuts:
        steps = jnp.exp(jax.random.uniform(jax.random.fold_in(own, axis_at), (parts,), jnp.float32, smallest / len(cuts), largest / len(cuts)))
        gain = gain * jnp.repeat(steps, dims[axis_at] // parts).reshape([-1 if axis == axis_at else 1 for axis in range(len(dims))])
    return gain


def split_up(number_of, total, limit, skew):
    portions = [(1 << 20) // math.isqrt(standing ** skew) + 1 for standing in range(2, number_of + 1)]
    spare, given = total - limit - (number_of - 1), [1] * (number_of - 1)
    while spare > 0:
        free = [i for i in range(number_of - 1) if given[i] < limit]
        whole, remaining = sum([portions[i] for i in free]), spare
        for i in free:
            extra = min(limit - given[i], max(1, remaining * portions[i] // whole), spare)
            given[i] = given[i] + extra
            spare = spare - extra
    return np.array([limit] + given)


def uneven(own_key, amount, total, bound, lean):
    if amount == 2:
        one = jax.random.randint(own_key, (), max(1, total - bound), min(bound, total - 1) + 1)
        return jnp.stack([one, total - one])
    tallies = jnp.asarray(split_up(amount, total, bound, lean), jnp.int32)
    couples = (amount - 1) // 2
    donor, taker = tallies[1:1 + 2 * couples:2], tallies[2:2 + 2 * couples:2]
    margin = jnp.minimum(donor - 1, bound - taker)
    shifted = jax.random.randint(jax.random.fold_in(own_key, 1), (couples,), 0, 1 << 20) % (margin + 1)
    tallies = tallies.at[1:1 + 2 * couples:2].set(donor - shifted).at[2:2 + 2 * couples:2].set(taker + shifted)
    return tallies[jax.random.permutation(jax.random.fold_in(own_key, 2), amount)]


def scatter_about(rng, extent, spread, most, pieces=(), held_as=jnp.bfloat16):
    loudness = level_of(rng, extent, pieces, -0.22, 0.18) if pieces else 1.0
    array = jax.random.normal(rng, extent, jnp.float32) * spread * loudness
    return jnp.minimum(jnp.maximum(array, -most), most).astype(held_as)


def setup_inputs(seed: int = 0) -> dict:
    key_list = jax.random.split(jax.random.key(seed), 10)
    return {
        "hidden": draw_hidden(jax.random.fold_in(key_list[9], 71), 0),
        "w_qkv": draw_w_qkv(jax.random.fold_in(key_list[9], 71), 0),
        "cond_vec": scatter_about(key_list[2], (D,), 1.0, 6.0),
        "head_w": scatter_about(key_list[3], (D,), D ** -0.5, 0.1875),
        "blocks": draw_blocks(jax.random.fold_in(key_list[9], 71), 0),
        "counts": jax.vmap(lambda own: uneven(own, NBLK, 2 * NBLK, NB - 1, 2))(jax.random.split(key_list[5], SEQS)).reshape((SEQS, NBLK)).astype(jnp.int32),
        "time_idx": place_ends(jax.random.randint(key_list[6], (SEQS, LEN), 0, STEPS), jax.random.fold_in(key_list[6], 1), 0, STEPS - 1).astype(jnp.int32),
        "cond_mask": place_ends((jax.random.randint(key_list[7], (SEQS, LEN), 0, 3) < 1).astype(jnp.int32), jax.random.fold_in(key_list[7], 1), 0, 1),
        "noise": scatter_about(key_list[8], (SEQS, LEN), 1.0, 6.0, ((0, 2), (1, 16)), jnp.float32),
    }


EPS = 1e-05

def time_features(steps_idx, width):
    half = width // 2
    freq = jnp.exp(-math.log(10000.0) * jnp.arange(half, dtype=jnp.float32) / half)
    angle = steps_idx.astype(jnp.float32)[:, None] * freq[None, :]
    return jnp.concatenate([jnp.sin(angle), jnp.cos(angle)], axis=1)

def reference(hidden, w_qkv, cond_vec, head_w, blocks, counts, time_idx, cond_mask, noise):
    scale = HD ** (-0.5)
    cond_row = cond_vec.astype(jnp.float32)
    head_row = head_w.astype(jnp.float32)
    weights_f = w_qkv

    def one_sequence(items):
        seq_hidden, seq_blocks, seq_counts, seq_time, seq_cond, seq_noise = items
        cond = seq_cond.astype(jnp.float32)
        h_in = seq_hidden.astype(jnp.float32) + cond[:, None] * cond_row[None, :] + time_features(seq_time, D)
        inv = lax.rsqrt(lax.optimization_barrier(jnp.mean(h_in * h_in, axis=1, keepdims=True)) + EPS)
        normed = (h_in * inv).astype(jnp.bfloat16)
        qkv = jnp.dot(normed, weights_f, preferred_element_type=jnp.float32).astype(jnp.bfloat16)
        query = qkv[:, :D].reshape(NBLK, BLK, H, HD)
        pairs = qkv[:, D:].reshape(NBLK, BLK, 2 * D)
        chosen = pairs[seq_blocks].reshape(NBLK, NB * BLK, 2, H, HD)
        keys = chosen[:, :, 0]
        vals = chosen[:, :, 1]
        valid = jnp.arange(NB, dtype=jnp.int32)[None, :] <= seq_counts[:, None]
        key_valid = jnp.repeat(valid, BLK, axis=1)
        scores = jnp.einsum('tqhd,tkhd->thqk', query.astype(jnp.float32), keys.astype(jnp.float32)) * scale
        scores = jnp.where(key_valid[:, None, None, :], scores, -1e+30)
        top = lax.optimization_barrier(jnp.max(scores, axis=3, keepdims=True))
        expo = jnp.exp(scores - top)
        probs = expo / lax.optimization_barrier(jnp.sum(expo, axis=3, keepdims=True))
        probs_b = probs.astype(jnp.bfloat16)
        attn = jnp.einsum('thqk,tkhd->tqhd', probs_b.astype(jnp.float32), vals.astype(jnp.float32)).astype(jnp.bfloat16)
        h_out = h_in + attn.reshape(LEN, D).astype(jnp.float32)
        net = lax.optimization_barrier(jnp.sum(h_out * head_row[None, :], axis=1))
        d_net = 2.0 * (1.0 - cond) * (net + seq_noise)
        d_out = d_net[:, None] * head_row[None, :]
        d_attn = d_out.astype(jnp.bfloat16).reshape(NBLK, BLK, H, HD)
        delta = lax.optimization_barrier(jnp.sum(d_attn.astype(jnp.float32) * attn.astype(jnp.float32), axis=3))
        d_probs = jnp.einsum('tqhd,tkhd->thqk', d_attn.astype(jnp.float32), vals.astype(jnp.float32))
        d_scores = (probs * (d_probs - jnp.transpose(delta, (0, 2, 1))[..., None])).astype(jnp.bfloat16)
        d_query = jnp.einsum('thqk,tkhd->tqhd', d_scores.astype(jnp.float32), keys.astype(jnp.float32)) * scale
        d_keys = jnp.einsum('thqk,tqhd->tkhd', d_scores.astype(jnp.float32), query.astype(jnp.float32)) * scale
        d_vals = jnp.einsum('thqk,tqhd->tkhd', probs_b.astype(jnp.float32), d_attn.astype(jnp.float32))
        d_chosen = jnp.stack([d_keys, d_vals], axis=2).reshape(NBLK * NB, BLK, 2 * D)
        d_pairs = jnp.zeros((NBLK, BLK, 2 * D), jnp.float32).at[seq_blocks.reshape(-1)].add(d_chosen)
        d_qkv = jnp.concatenate([d_query.reshape(LEN, D), d_pairs.reshape(LEN, 2 * D)], axis=1).astype(jnp.bfloat16)
        grad = jnp.dot(normed.T, d_qkv, preferred_element_type=jnp.float32)
        d_normed = jnp.dot(d_qkv, weights_f.T, preferred_element_type=jnp.float32)
        d_in = inv * (d_normed - h_in * inv * inv * lax.optimization_barrier(jnp.mean(d_normed * h_in, axis=1, keepdims=True)))
        return ((d_out + d_in).astype(jnp.bfloat16), grad)
    d_hidden, grads = lax.map(one_sequence, (hidden, blocks, counts, time_idx, cond_mask, noise))
    return (d_hidden, lax.optimization_barrier(jnp.sum(grads, axis=0)))
```

```python
import functools
import math

import jax
import jax.numpy as jnp
from jax import lax
from jax.experimental import pallas as pl
from jax.experimental.pallas import tpu as pltpu
from jax.sharding import PartitionSpec as P

HD = 64
BLK = 64
REACH = 4
NB = 5
PAIR = 2 * HD
GROUP = 4
EPS = 1e-05
SCALE = HD ** (-0.5)
NEG = -1e30
F32 = jnp.float32
BF16 = jnp.bfloat16
MESH = pl.DeviceIdType.MESH
ANY = pl.BlockSpec(memory_space=pl.ANY)
VMEM = pl.BlockSpec(memory_space=pltpu.VMEM)


def dot_nt(a, b):
    return lax.dot_general(a, b, (((1,), (1,)), ((), ())), preferred_element_type=F32)


def dot_tn(a, b):
    return lax.dot_general(a, b, (((0,), (0,)), ((), ())), preferred_element_type=F32)


def dot_nn(a, b):
    return jnp.dot(a, b, preferred_element_type=F32)


class Place:
    def __init__(self):
        seq = lax.axis_index("seq")
        self.f = lax.axis_index("fsdp")
        self.z = seq // GROUP
        self.g = seq % GROUP
        self.core = self.g % 2
        self.x = self.g // 2
        self.g_core = self.x * 2 + 1 - self.core
        self.g_x = (1 - self.x) * 2 + self.core
        self.g_far = (1 - self.x) * 2 + 1 - self.core

    def at(self, z=None, g=None, f=None):
        z = self.z if z is None else z
        g = self.g if g is None else g
        f = self.f if f is None else f
        return (z * GROUP + g, f)


def remote(src, dst, send, recv, device):
    return pltpu.make_async_remote_copy(
        src_ref=src, dst_ref=dst, send_sem=send, recv_sem=recv, device_id=device, device_id_type=MESH
    )


def greet(devices):
    barrier = pltpu.get_barrier_semaphore()
    for device in devices:
        pl.semaphore_signal(barrier, inc=1, device_id=device, device_id_type=MESH)
    return barrier


def front_kernel(
    nf,
    nz,
    hidden_ref,
    w_ref,
    rows_ref,
    cvec_ref,
    head_ref,
    freq_ref,
    seen_ref,
    qkv_out,
    norm_out,
    seen_out,
    w_out,
    hin_out,
    base_out,
    nbuf,
    wbuf,
    hbuf,
    qbuf,
    cols,
    base,
    w_send,
    w_recv,
    w_own,
    n_send,
    n_recv,
    o_sem,
    q_sem,
):
    me = Place()
    tokens, width = hidden_ref.shape
    gw = width // GROUP
    rows = w_ref.shape[0]
    last = GROUP - 1
    first_g = me.g == 0
    last_g = me.g == last
    halo_from = me.at(
        z=jnp.where(me.core == 1, (me.z + nz - 1) % nz, (me.z + 1) % nz),
        g=jnp.where(me.core == 1, last, 0),
    )
    f_peers = [me.at(f=(me.f + o) % nf) for o in range(1, nf)]
    barrier = greet(f_peers + [me.at(g=me.g_x), me.at(g=me.g_core), halo_from])
    at_edge = jnp.logical_or(first_g, last_g)

    @pl.when(at_edge)
    def _():
        pl.semaphore_wait(barrier, nf + 3)

    @pl.when(jnp.logical_not(at_edge))
    def _():
        pl.semaphore_wait(barrier, nf + 1)

    own_rows = pl.ds(pl.multiple_of(me.f * rows, rows), rows)
    w_copies = []
    own_copies = []
    for j in range(3):
        src = w_ref.at[:, pl.ds(pl.multiple_of(j * width + me.g * gw, gw), gw)]
        for o in range(1, nf):
            at = (o - 1) * 3 + j
            copy = remote(
                src, wbuf.at[own_rows, j * gw : (j + 1) * gw], w_send.at[at], w_recv.at[at], f_peers[o - 1]
            )
            copy.start()
            w_copies.append(copy)
    for j in range(3):
        src = w_ref.at[:, pl.ds(pl.multiple_of(j * width + me.g * gw, gw), gw)]
        copy = pltpu.make_async_copy(src, wbuf.at[own_rows, j * gw : (j + 1) * gw], w_own.at[j])
        copy.start()
        own_copies.append(copy)

    slot = me.g + 1
    cols[...] = rows_ref[...].T
    step = 32

    def token_tile(i, carry):
        at = pl.ds(pl.multiple_of(i * step, step), step)
        angle = cols[at, 0:1] * freq_ref[...]
        feats = jnp.concatenate([jnp.sin(angle), jnp.cos(angle)], axis=1)
        h_in = hidden_ref[at, :].astype(F32) + cols[at, 1:2] * cvec_ref[...] + feats
        inv = lax.rsqrt(jnp.mean(h_in * h_in, axis=1, keepdims=True) + EPS)
        hbuf[at, :] = h_in
        nbuf[slot, at, :] = (h_in * inv).astype(BF16)
        base[at, :] = jnp.broadcast_to(jnp.sum(h_in * head_ref[...], axis=1, keepdims=True), (step, 128))
        return carry

    lax.fori_loop(0, tokens // step, token_tile, 0)
    nbuf[slot, tokens:, :] = seen_ref[...]

    def moved(slot_at, to, send, recv):
        return remote(nbuf.at[slot_at], nbuf.at[slot_at], n_send.at[send], n_recv.at[recv], to)

    own_x = moved(slot, me.at(g=me.g_x), 0, 0)
    own_x.start()
    next_z = (me.z + 1) % nz
    prev_z = (me.z + nz - 1) % nz

    def halo_copies(dst, z, core):
        return [
            remote(nbuf.at[slot], nbuf.at[dst], n_send.at[3 + x], n_recv.at[3], me.at(z=z, g=2 * x + core))
            for x in range(2)
        ]

    @pl.when(last_g)
    def _():
        for copy in halo_copies(0, next_z, 1):
            copy.start()

    @pl.when(first_g)
    def _():
        for copy in halo_copies(GROUP + 1, prev_z, 0):
            copy.start()

    to_core = me.at(g=me.g_core)
    own_core = moved(slot, to_core, 1, 1)
    own_core.start()

    hin_copy = pltpu.make_async_copy(hbuf, hin_out, o_sem.at[0])
    hin_copy.start()
    base_out[...] = base[...].T[:8, :]

    for copy in own_copies:
        copy.wait()
    for copy in w_copies:
        copy.wait()
    w_copy = pltpu.make_async_copy(wbuf, w_out, o_sem.at[1])
    w_copy.start()

    def project(slot_at, at):
        qbuf[slot_at] = dot_nn(nbuf[slot_at, :tokens, :], wbuf[...]).astype(BF16)
        pltpu.make_async_copy(qbuf.at[slot_at], qkv_out.at[slot_at], q_sem.at[at]).start()

    project(slot, 0)
    core_slot = me.g_core + 1
    moved(core_slot, to_core, 1, 1).wait_recv()
    project(core_slot, 1)
    x_slot = me.g_x + 1
    moved(x_slot, to_core, 0, 0).wait_recv()
    x_core = moved(x_slot, to_core, 2, 2)
    x_core.start()
    project(x_slot, 2)
    far_slot = me.g_far + 1
    moved(far_slot, to_core, 2, 2).wait_recv()
    project(far_slot, 3)
    near_halo = jnp.where(me.core == 1, 0, GROUP + 1)
    other_halo = jnp.where(me.core == 1, GROUP + 1, 0)
    moved(near_halo, to_core, 3, 3).wait_recv()
    halo_core = moved(near_halo, to_core, 5, 4)
    halo_core.start()
    norm_copies = []
    for j in range(GROUP):
        copy = pltpu.make_async_copy(nbuf.at[1 + j, :tokens, :], norm_out.at[j], o_sem.at[2 + j])
        copy.start()
        norm_copies.append(copy)
    project(near_halo, 4)
    moved(other_halo, to_core, 5, 4).wait_recv()
    project(other_halo, 5)
    seen_out[...] = nbuf[:, tokens:, : 2 * PAIR]

    own_x.wait_send()
    own_core.wait_send()
    x_core.wait_send()
    halo_core.wait_send()

    @pl.when(last_g)
    def _():
        for copy in halo_copies(0, next_z, 1):
            copy.wait_send()

    @pl.when(first_g)
    def _():
        for copy in halo_copies(GROUP + 1, prev_z, 0):
            copy.wait_send()

    hin_copy.wait()
    w_copy.wait()
    for copy in norm_copies:
        copy.wait()
    for at in range(GROUP + 2):
        pltpu.make_async_copy(qbuf.at[at], qkv_out.at[at], q_sem.at[at]).wait()


def front_call(nf, nz, hidden, w, rows, cvec, head_row, freq, seen):
    tokens, width = hidden.shape
    gw = width // GROUP
    slots = GROUP + 2
    return pl.pallas_call(
        functools.partial(front_kernel, nf, nz),
        in_specs=[VMEM, ANY, VMEM, VMEM, VMEM, VMEM, VMEM],
        out_specs=[ANY, ANY, VMEM, ANY, ANY, VMEM],
        out_shape=[
            jax.ShapeDtypeStruct((slots, tokens, 3 * gw), BF16),
            jax.ShapeDtypeStruct((GROUP, tokens, width), BF16),
            jax.ShapeDtypeStruct((slots, 16, 2 * PAIR), BF16),
            jax.ShapeDtypeStruct((width, 3 * gw), BF16),
            jax.ShapeDtypeStruct((tokens, width), F32),
            jax.ShapeDtypeStruct((8, tokens), F32),
        ],
        scratch_shapes=[
            pltpu.VMEM((slots, tokens + 16, width), BF16),
            pltpu.VMEM((width, 3 * gw), BF16),
            pltpu.VMEM((tokens, width), F32),
            pltpu.VMEM((slots, tokens, 3 * gw), BF16),
            pltpu.VMEM((tokens, 128), F32),
            pltpu.VMEM((tokens, 128), F32),
            pltpu.SemaphoreType.DMA((3 * (nf - 1),)),
            pltpu.SemaphoreType.DMA((3 * (nf - 1),)),
            pltpu.SemaphoreType.DMA((3,)),
            pltpu.SemaphoreType.DMA((6,)),
            pltpu.SemaphoreType.DMA((5,)),
            pltpu.SemaphoreType.DMA((2 + GROUP,)),
            pltpu.SemaphoreType.DMA((slots,)),
        ],
        compiler_params=pltpu.CompilerParams(
            collective_id=0, has_side_effects=True, vmem_limit_bytes=40 << 20
        ),
        name="front",
    )(hidden, w, rows, cvec, head_row, freq, seen)


def block_rows(seen, count, tokens):
    at = lax.broadcasted_iota(jnp.int32, (PAIR, tokens), 0)
    of = lax.broadcasted_iota(jnp.int32, (PAIR, tokens), 1) // BLK
    return dot_nn(seen, jnp.where(at == of, 1.0, 0.0).astype(BF16))


def spread(rows):
    return jnp.concatenate(
        [jnp.broadcast_to(rows[b : b + 1], (BLK, rows.shape[1])) for b in range(rows.shape[0])], axis=0
    )


def forward_kernel(qkv_ref, seen_ref, head_ref, attn_ref, stats_ref, net_ref):
    i = pl.program_id(0)
    tokens = attn_ref.shape[0]
    gw = attn_ref.shape[1]
    window = 3 * tokens
    blocks = tokens // BLK
    lane = lax.broadcasted_iota(jnp.int32, (1, PAIR), 1)
    visible = block_rows(seen_ref[i + 1, :, :PAIR], blocks, window)[:blocks]
    bias = spread(jnp.where(visible > 0.5, 0.0, NEG))
    stats = jnp.zeros(stats_ref.shape, F32)
    net = jnp.zeros(net_ref.shape, F32)
    for pair in range(gw // PAIR):
        part = slice(pair * PAIR, (pair + 1) * PAIR)
        query = qkv_ref[i + 1, :, part] * jnp.asarray(SCALE, BF16)
        keys = qkv_ref[pl.ds(i, 3), :, gw + pair * PAIR : gw + (pair + 1) * PAIR].reshape(window, PAIR)
        vals = qkv_ref[pl.ds(i, 3), :, 2 * gw + pair * PAIR : 2 * gw + (pair + 1) * PAIR].reshape(window, PAIR)
        outs = []
        for half in range(2):
            mine = (lane < HD) if half == 0 else (lane >= HD)
            scores = dot_nt(jnp.where(mine, query, jnp.zeros_like(query)), keys) + bias
            top = jnp.max(scores, axis=1, keepdims=True)
            expo = jnp.exp(scores - top)
            total = jnp.sum(expo, axis=1, keepdims=True)
            probs_b = (expo * (1.0 / total)).astype(BF16)
            outs.append(dot_nn(probs_b, vals))
            stats = jnp.where(lane == 2 * pair + half, top + jnp.log(total), stats)
        attn = jnp.where(lane < HD, outs[0], outs[1]).astype(BF16)
        attn_ref[:, part] = attn
        net = net + dot_nt(head_ref[:, part], attn)
    stats_ref[...] = stats
    net_ref[...] = net


def forward_call(qkv, seen, head_rows):
    slots, tokens, cols = qkv.shape
    gw = cols // 3
    total = GROUP * tokens
    return pl.pallas_call(
        forward_kernel,
        grid=(GROUP,),
        in_specs=[
            pl.BlockSpec(qkv.shape, lambda i: (0, 0, 0)),
            pl.BlockSpec(seen.shape, lambda i: (0, 0, 0)),
            pl.BlockSpec(head_rows.shape, lambda i: (0, 0)),
        ],
        out_specs=[
            pl.BlockSpec((tokens, gw), lambda i: (i, 0)),
            pl.BlockSpec((tokens, PAIR), lambda i: (i, 0)),
            pl.BlockSpec((head_rows.shape[0], tokens), lambda i: (0, i)),
        ],
        out_shape=[
            jax.ShapeDtypeStruct((total, gw), BF16),
            jax.ShapeDtypeStruct((total, PAIR), F32),
            jax.ShapeDtypeStruct((head_rows.shape[0], total), F32),
        ],
        compiler_params=pltpu.CompilerParams(vmem_limit_bytes=48 << 20),
        name="attn_forward",
    )(qkv, seen, head_rows)


def exchange_kernel(
    nz,
    net_ref,
    base_ref,
    rows_ref,
    stats_ref,
    attn_ref,
    head_ref,
    stats_out,
    rows_out,
    dattn_out,
    mbuf,
    rbuf,
    m_send,
    m_recv,
    r_send,
    r_recv,
):
    me = Place()
    total = stats_ref.shape[0]
    tokens = total // GROUP
    gw = attn_ref.shape[1]
    peers = [me.at(g=(me.g + o) % GROUP) for o in range(1, GROUP)]
    next_z = me.at(z=(me.z + 1) % nz)
    prev_z = me.at(z=(me.z + nz - 1) % nz)
    barrier = greet(peers + [next_z, prev_z])
    pl.semaphore_wait(barrier, GROUP + 1)

    own = pl.ds(pl.multiple_of(me.g * tokens, tokens), tokens)
    at_row = lax.broadcasted_iota(jnp.int32, (8, total), 0)
    mbuf[0] = jnp.where(at_row == 0, net_ref[:8, :], 0.0)
    own_row = lax.broadcasted_iota(jnp.int32, (8, tokens), 0)
    extra = jnp.where(
        own_row == 0,
        base_ref[0:1, :] + rows_ref[2:3, :],
        jnp.where(own_row == 1, 2.0 * (1.0 - rows_ref[1:2, :]), 0.0),
    )
    mbuf[0, :, own] = mbuf[0, :, own] + extra
    copies = []
    for o in range(1, GROUP):
        copy = remote(mbuf.at[0], mbuf.at[o], m_send.at[o - 1], m_recv.at[o - 1], peers[o - 1])
        copy.start()
        copies.append(copy)
    for copy in copies:
        copy.wait()
    msg = mbuf[0] + mbuf[1] + mbuf[2] + mbuf[3]
    d_net = msg[0:1, :] * msg[1:2, :]

    lane = lax.broadcasted_iota(jnp.int32, (1, PAIR), 1)

    def grads(row):
        col = jnp.broadcast_to(row, (PAIR, row.shape[1])).T
        return col, [
            (col * head_ref[0:1, p * PAIR : (p + 1) * PAIR]).astype(BF16) for p in range(gw // PAIR)
        ]

    col, parts = grads(d_net)
    full = jnp.where(lane == 8, col, stats_ref[...])
    for p, d_attn in enumerate(parts):
        dattn_out[tokens : tokens + total, p * PAIR : (p + 1) * PAIR] = d_attn
        prod = d_attn.astype(F32) * attn_ref[:, p * PAIR : (p + 1) * PAIR].astype(F32)
        low = jnp.sum(jnp.where(lane < HD, prod, 0.0), axis=1, keepdims=True)
        high = jnp.sum(jnp.where(lane < HD, 0.0, prod), axis=1, keepdims=True)
        full = jnp.where(lane == 4 + 2 * p, low, full)
        full = jnp.where(lane == 5 + 2 * p, high, full)
    stats_out[...] = full
    rows = full.T[:16, :]
    for j in range(GROUP):
        rbuf[1 + j] = rows[:, j * tokens : (j + 1) * tokens]
    right = remote(rbuf.at[GROUP], rbuf.at[0], r_send.at[0], r_recv.at[0], next_z)
    left = remote(rbuf.at[1], rbuf.at[GROUP + 1], r_send.at[1], r_recv.at[1], prev_z)
    right.start()
    left.start()
    right.wait()
    left.wait()
    for j in range(GROUP + 2):
        rows_out[:, j * tokens : (j + 1) * tokens] = rbuf[j]
    for j in (0, GROUP + 1):
        unused, parts = grads(rbuf[j][8:9, :])
        for p, d_attn in enumerate(parts):
            dattn_out[j * tokens : (j + 1) * tokens, p * PAIR : (p + 1) * PAIR] = d_attn


def exchange_call(nz, net, base, rows, stats, attn, head_group):
    total = stats.shape[0]
    tokens = total // GROUP
    gw = attn.shape[1]
    return pl.pallas_call(
        functools.partial(exchange_kernel, nz),
        in_specs=[VMEM] * 6,
        out_specs=[VMEM] * 3,
        out_shape=[
            jax.ShapeDtypeStruct(stats.shape, F32),
            jax.ShapeDtypeStruct((16, total + 2 * tokens), F32),
            jax.ShapeDtypeStruct((total + 2 * tokens, gw), BF16),
        ],
        scratch_shapes=[
            pltpu.VMEM((GROUP, 8, total), F32),
            pltpu.VMEM((GROUP + 2, 16, tokens), F32),
            pltpu.SemaphoreType.DMA((GROUP - 1,)),
            pltpu.SemaphoreType.DMA((GROUP - 1,)),
            pltpu.SemaphoreType.DMA((2,)),
            pltpu.SemaphoreType.DMA((2,)),
        ],
        compiler_params=pltpu.CompilerParams(
            collective_id=1, has_side_effects=True, vmem_limit_bytes=32 << 20
        ),
        name="stats_exchange",
    )(net, base, rows, stats, attn, head_group)


def backward_kernel(qkv_ref, seen_ref, stats_ref, rows_ref, dattn_ref, d_qkv_ref):
    i = pl.program_id(0)
    tokens = d_qkv_ref.shape[0]
    gw = d_qkv_ref.shape[1] // 3
    window = 3 * tokens
    blocks = tokens // BLK
    lane = lax.broadcasted_iota(jnp.int32, (1, PAIR), 1)
    low = lane < HD
    visible = block_rows(seen_ref[i + 1, :, :PAIR], blocks, window)[:blocks]
    bias = spread(jnp.where(visible > 0.5, 0.0, NEG))
    visible_t = jnp.concatenate(
        [
            block_rows(seen_ref[i + s, :, PAIR:], blocks, tokens)[(2 - s) * blocks : (3 - s) * blocks]
            for s in range(3)
        ],
        axis=1,
    )
    bias_t = spread(jnp.where(visible_t > 0.5, 0.0, NEG))
    stats = stats_ref[...]
    at = pl.ds(pl.multiple_of(i * tokens, tokens), window)
    own_at = pl.ds(pl.multiple_of((i + 1) * tokens, tokens), tokens)
    for pair in range(gw // PAIR):
        part = slice(pair * PAIR, (pair + 1) * PAIR)
        k_part = slice(gw + pair * PAIR, gw + (pair + 1) * PAIR)
        v_part = slice(2 * gw + pair * PAIR, 2 * gw + (pair + 1) * PAIR)
        scale = jnp.asarray(SCALE, BF16)
        query = qkv_ref[pl.ds(i, 3), :, part].reshape(window, PAIR) * scale
        own_query = qkv_ref[i + 1, :, part] * scale
        keys = qkv_ref[pl.ds(i, 3), :, k_part].reshape(window, PAIR)
        vals = qkv_ref[pl.ds(i, 3), :, v_part].reshape(window, PAIR)
        own_keys = qkv_ref[i + 1, :, k_part]
        own_vals = qkv_ref[i + 1, :, v_part]
        d_attn = dattn_ref[at, part]
        own_d_attn = dattn_ref[own_at, part]
        d_q, d_k, d_v = [], [], []
        for half in range(2):
            mine = low if half == 0 else jnp.logical_not(low)
            head = 2 * pair + half
            lse = stats[:, head : head + 1]
            delta = stats[:, 4 + head : 5 + head]
            probs = jnp.exp(dot_nt(jnp.where(mine, own_query, jnp.zeros_like(own_query)), keys) + bias - lse)
            d_probs = dot_nt(jnp.where(mine, own_d_attn, jnp.zeros_like(own_d_attn)), vals)
            d_scores = (probs * (d_probs - delta)).astype(BF16)
            d_q.append(dot_nn(d_scores, keys))
            lse_row = rows_ref[head : head + 1, at]
            delta_row = rows_ref[4 + head : 5 + head, at]
            own_keys_m = jnp.where(mine, own_keys, jnp.zeros_like(own_keys))
            own_vals_m = jnp.where(mine, own_vals, jnp.zeros_like(own_vals))
            probs_t = jnp.exp(dot_nt(own_keys_m, query) + bias_t - lse_row)
            d_v.append(dot_nn(probs_t.astype(BF16), d_attn))
            d_probs_t = dot_nt(own_vals_m, d_attn)
            d_scores_t = (probs_t * (d_probs_t - delta_row)).astype(BF16)
            d_k.append(dot_nn(d_scores_t, query))
        d_qkv_ref[:, part] = (jnp.where(low, d_q[0], d_q[1]) * SCALE).astype(BF16)
        d_qkv_ref[:, k_part] = jnp.where(low, d_k[0], d_k[1]).astype(BF16)
        d_qkv_ref[:, v_part] = jnp.where(low, d_v[0], d_v[1]).astype(BF16)


def backward_call(qkv, seen, stats, rows, dattn):
    slots, tokens, cols = qkv.shape
    return pl.pallas_call(
        backward_kernel,
        grid=(GROUP,),
        in_specs=[
            pl.BlockSpec(qkv.shape, lambda i: (0, 0, 0)),
            pl.BlockSpec(seen.shape, lambda i: (0, 0, 0)),
            pl.BlockSpec((tokens, PAIR), lambda i: (i, 0)),
            pl.BlockSpec(rows.shape, lambda i: (0, 0)),
            pl.BlockSpec(dattn.shape, lambda i: (0, 0)),
        ],
        out_specs=pl.BlockSpec((tokens, cols), lambda i: (i, 0)),
        out_shape=jax.ShapeDtypeStruct((GROUP * tokens, cols), BF16),
        compiler_params=pltpu.CompilerParams(vmem_limit_bytes=48 << 20),
        name="attn_backward",
    )(qkv, seen, stats, rows, dattn)


def grad_kernel(
    nf,
    nz,
    nr,
    d_qkv_ref,
    norm_ref,
    w_ref,
    hin_ref,
    stats_ref,
    head_ref,
    grad_out,
    d_hidden_out,
    acc,
    y_buf,
    y_got,
    z_buf,
    z_got,
    res,
    dn_acc,
    dn_buf,
    dn_got,
    y_send,
    y_recv,
    z_send,
    z_recv,
    a_send,
    a_recv,
    g_send,
    g_recv,
    d_send,
    d_recv,
    o_sem,
):
    me = Place()
    tokens, width = hin_ref.shape
    total = d_qkv_ref.shape[0]
    gw = d_qkv_ref.shape[1] // 3
    rows = width // nf
    rc = rows // nr
    zr = rc // nz
    chunks = 3 * nr
    f_peers = [me.at(f=(me.f + o) % nf) for o in range(1, nf)]
    z_peers = [me.at(z=(me.z + o) % nz) for o in range(1, nz)]
    to_x = me.at(g=me.g_x)
    to_core = me.at(g=me.g_core)
    barrier = greet(f_peers + z_peers + [to_x, to_core])
    pl.semaphore_wait(barrier, nf + nz)

    def product(f, j):
        at = pl.ds(pl.multiple_of(f * rows, rows), rows)
        lhs = norm_ref[:, :, at].reshape(total, rows)
        return dot_tn(lhs, d_qkv_ref[:, j * gw : (j + 1) * gw])

    y_copies = []
    for j in range(3):
        for o in range(1, nf):
            part = product((me.f + o) % nf, j).astype(BF16)
            for r in range(nr):
                k = j * nr + r
                y_buf[o - 1, k] = part[r * rc : (r + 1) * rc]
                copy = remote(
                    y_buf.at[o - 1, k], y_got.at[o - 1, k], y_send.at[o - 1, k], y_recv.at[o - 1, k], f_peers[o - 1]
                )
                copy.start()
                y_copies.append(copy)

    def d_normed(g):
        at = pl.ds(pl.multiple_of(g * tokens, tokens), tokens)
        return dot_nt(d_qkv_ref[at, :], w_ref[...])

    d_copies = []
    for at, g in enumerate((me.g_far, me.g_core)):
        dn_buf[at] = d_normed(g).astype(BF16)
        copy = remote(dn_buf.at[at], dn_got.at[at], d_send.at[at], d_recv.at[at], to_core)
        copy.start()
        d_copies.append(copy)
    dn_x = d_normed(me.g_x)
    d_copies[0].wait_recv()
    dn_buf[2] = (dn_x + dn_got[0].astype(F32)).astype(BF16)
    copy = remote(dn_buf.at[2], dn_got.at[2], d_send.at[2], d_recv.at[2], to_x)
    copy.start()
    d_copies.append(copy)
    for j in range(3):
        part = product(me.f, j)
        for r in range(nr):
            acc[j * nr + r] = part[r * rc : (r + 1) * rc]
    dn_acc[...] = d_normed(me.g)

    def z_copy(k, o):
        to = (me.z + o) % nz
        at = pl.ds(pl.multiple_of(to * zr, zr), zr)
        return remote(z_buf.at[k, at, :], z_got.at[o - 1, k], z_send.at[o - 1, k], z_recv.at[o - 1, k], z_peers[o - 1])

    z_own = pl.ds(pl.multiple_of(me.z * zr, zr), zr)

    def a_copy(k, o):
        ref = res.at[me.g, k, z_own, :]
        return remote(ref, ref, a_send.at[o - 1, k], a_recv.at[o - 1, k], z_peers[o - 1])

    def g_copy(g, k, way, to):
        return remote(res.at[g, k], res.at[g, k], g_send.at[way, k], g_recv.at[way, k], to)

    def out_copy(g, k):
        j, r = k // nr, k % nr
        at = pl.ds(pl.multiple_of(j * width + g * gw, gw), gw)
        return pltpu.make_async_copy(res.at[g, k], grad_out.at[r * rc : (r + 1) * rc, at], o_sem.at[g, k])

    def stage_a(k):
        value = acc[k]
        for o in range(1, nf):
            remote(
                y_buf.at[o - 1, k], y_got.at[o - 1, k], y_send.at[o - 1, k], y_recv.at[o - 1, k], f_peers[o - 1]
            ).wait_recv()
            value = value + y_got[o - 1, k].astype(F32)
        acc[k] = value
        z_buf[k] = value.astype(BF16)
        for o in range(1, nz):
            z_copy(k, o).start()

    def stage_b(k):
        value = acc[k, z_own, :]
        for o in range(1, nz):
            z_copy(k, o).wait_recv()
            value = value + z_got[o - 1, k].astype(F32)
        res[me.g, k, z_own, :] = value.astype(BF16)
        for o in range(1, nz):
            a_copy(k, o).start()

    def stage_c(k):
        for o in range(1, nz):
            a_copy(k, o).wait_recv()
        g_copy(me.g, k, 0, to_x).start()
        g_copy(me.g, k, 1, to_core).start()
        out_copy(me.g, k).start()

    def stage_d(k):
        g_copy(me.g_x, k, 0, to_x).wait_recv()
        g_copy(me.g_x, k, 2, to_core).start()
        out_copy(me.g_x, k).start()

    def stage_e(k):
        g_copy(me.g_core, k, 1, to_core).wait_recv()
        out_copy(me.g_core, k).start()
        g_copy(me.g_far, k, 2, to_core).wait_recv()
        out_copy(me.g_far, k).start()

    stages = (stage_a, stage_b, stage_c, stage_d, stage_e)
    for t in range(chunks + len(stages) - 1):
        for lag, stage in enumerate(stages):
            if 0 <= t - lag < chunks:
                stage(t - lag)
        if t == chunks - 2:
            d_copies[1].wait_recv()
            d_copies[2].wait_recv()
            d_norm = dn_acc[...] + dn_got[1].astype(F32) + dn_got[2].astype(F32)
            h_in = hin_ref[...]
            inv = lax.rsqrt(jnp.mean(h_in * h_in, axis=1, keepdims=True) + EPS)
            own = pl.ds(pl.multiple_of(me.g * tokens, tokens), tokens)
            d_out = stats_ref[own, 8:9] * head_ref[...]
            mean = jnp.mean(d_norm * h_in, axis=1, keepdims=True)
            d_hidden_out[...] = (d_out + inv * (d_norm - h_in * inv * inv * mean)).astype(BF16)

    for copy in y_copies + d_copies:
        copy.wait_send()
    for k in range(chunks):
        for o in range(1, nz):
            z_copy(k, o).wait_send()
            a_copy(k, o).wait_send()
        g_copy(me.g, k, 0, to_x).wait_send()
        g_copy(me.g, k, 1, to_core).wait_send()
        g_copy(me.g_x, k, 2, to_core).wait_send()
        for g in range(GROUP):
            out_copy(g, k).wait()


def grad_call(nf, nz, d_qkv, normed, w_group, h_in, stats, head_row):
    tokens, width = h_in.shape
    gw = d_qkv.shape[1] // 3
    rows = width // nf
    nr = 2 if rows % (32 * nz) == 0 else 1
    rc = rows // nr
    zr = rc // nz
    chunks = 3 * nr
    dma = pltpu.SemaphoreType.DMA
    return pl.pallas_call(
        functools.partial(grad_kernel, nf, nz, nr),
        in_specs=[VMEM] * 6,
        out_specs=[ANY, VMEM],
        out_shape=[
            jax.ShapeDtypeStruct((rows, GROUP * 3 * gw), BF16),
            jax.ShapeDtypeStruct((tokens, width), BF16),
        ],
        scratch_shapes=[
            pltpu.VMEM((chunks, rc, gw), F32),
            pltpu.VMEM((nf - 1, chunks, rc, gw), BF16),
            pltpu.VMEM((nf - 1, chunks, rc, gw), BF16),
            pltpu.VMEM((chunks, rc, gw), BF16),
            pltpu.VMEM((nz - 1, chunks, zr, gw), BF16),
            pltpu.VMEM((GROUP, chunks, rc, gw), BF16),
            pltpu.VMEM((tokens, width), F32),
            pltpu.VMEM((3, tokens, width), BF16),
            pltpu.VMEM((3, tokens, width), BF16),
            dma((nf - 1, chunks)),
            dma((nf - 1, chunks)),
            dma((nz - 1, chunks)),
            dma((nz - 1, chunks)),
            dma((nz - 1, chunks)),
            dma((nz - 1, chunks)),
            dma((3, chunks)),
            dma((3, chunks)),
            dma((3,)),
            dma((3,)),
            dma((GROUP, chunks)),
        ],
        compiler_params=pltpu.CompilerParams(
            collective_id=2, has_side_effects=True, vmem_limit_bytes=48 << 20
        ),
        name="grad_reduce",
    )(d_qkv, normed, w_group, h_in, stats, head_row)


def body(hidden, w_qkv, cond_vec, head_w, blocks, counts, time_idx, cond_mask, noise):
    tokens, width = hidden.shape[1:]
    gw = width // GROUP
    nf = lax.axis_size("fsdp")
    nz = lax.axis_size("seq") // GROUP
    local = tokens // BLK
    seq = lax.axis_index("seq")
    first = seq * local
    total_blocks = local * lax.axis_size("seq")

    used = lax.broadcasted_iota(jnp.int32, (local, NB), 1) <= counts[0][:, None]
    place = jnp.where(used, jnp.remainder(blocks[0] - (first - local) + total_blocks, total_blocks), -1)
    seen = jnp.any(place[:, :, None] == jnp.arange(3 * local, dtype=jnp.int32)[None, None, :], axis=1)
    seen = seen.astype(BF16)
    seen_rows = jnp.concatenate(
        [
            jnp.pad(seen, ((0, 16 - local), (0, PAIR - 3 * local))),
            jnp.pad(seen.T, ((0, 16 - 3 * local), (0, PAIR - local))),
            jnp.zeros((16, width - 2 * PAIR), BF16),
        ],
        axis=1,
    )
    head_row = head_w.astype(F32)[None, :]
    half = width // 2
    freq = jnp.exp(-math.log(10000.0) * jnp.arange(half, dtype=F32) / half)[None, :]
    rows = jnp.concatenate(
        [time_idx.astype(F32), cond_mask.astype(F32), noise, jnp.zeros((125, tokens), F32)], axis=0
    )
    qkv, normed, seen_ext, w_group, h_in, base = front_call(
        nf, nz, hidden[0], w_qkv, rows, cond_vec.astype(F32)[None, :], head_row, freq, seen_rows
    )
    g = seq % GROUP
    head_group = lax.dynamic_slice_in_dim(head_w, g * gw, gw)
    head_rows = jnp.broadcast_to(head_group[None, :], (16, gw))
    attn, stats, net = forward_call(qkv, seen_ext, head_rows)
    stats, rows_ext, dattn = exchange_call(
        nz, net, base, rows, stats, attn, jnp.broadcast_to(head_group.astype(F32)[None, :], (8, gw))
    )
    d_qkv = backward_call(qkv, seen_ext, stats, rows_ext, dattn)
    grad, d_hidden = grad_call(nf, nz, d_qkv, normed, w_group, h_in, stats, head_row)
    return (d_hidden[None], grad.astype(F32))


def solution(mesh):
    return jax.shard_map(
        body,
        mesh=mesh,
        in_specs=(
            P("fsdp", "seq", None),
            P("fsdp", None),
            P(),
            P(),
            P("fsdp", "seq", None),
            P("fsdp", "seq"),
            P("fsdp", "seq"),
            P("fsdp", "seq"),
            P("fsdp", "seq"),
        ),
        out_specs=(P("fsdp", "seq", None), P("fsdp", None)),
        check_vma=False,
    )
```

```python
import functools
import math

import jax
import jax.numpy as jnp
import numpy as np
from jax import lax
from jax.experimental import pallas as pl
from jax.experimental.pallas import tpu as pltpu
from jax.sharding import PartitionSpec as P

HD = 64
BLK = 64
PAIR = 2 * HD
TRIO = 3 * PAIR
GROUP = 4
PAIRS = 2
SLOTS = GROUP + 2
SPLIT = 2
EPS = 1e-05
SCALE = HD ** (-0.5)
NEG = -1e30
F32 = jnp.float32
BF16 = jnp.bfloat16
MESH = pl.DeviceIdType.MESH
ANY = pl.BlockSpec(memory_space=pl.ANY)
VMEM = pl.BlockSpec(memory_space=pltpu.VMEM)
SMEM = pl.BlockSpec(memory_space=pltpu.SMEM)


def dot_nt(a, b):
    return lax.dot_general(a, b, (((1,), (1,)), ((), ())), preferred_element_type=F32)


def dot_nn(a, b):
    return jnp.dot(a, b, preferred_element_type=F32)


class Place:
    def __init__(self):
        seq = lax.axis_index("seq")
        self.seq = seq
        self.f = lax.axis_index("fsdp")
        self.z = seq // GROUP
        self.g = seq % GROUP
        self.core = self.g % 2
        self.x = self.g // 2
        self.g_core = self.x * 2 + 1 - self.core
        self.g_x = (1 - self.x) * 2 + self.core
        self.g_far = (1 - self.x) * 2 + 1 - self.core

    def at(self, z=None, g=None, f=None):
        z = self.z if z is None else z
        g = self.g if g is None else g
        f = self.f if f is None else f
        return (z * GROUP + g, f)


def remote(src, dst, send, recv, device):
    return pltpu.make_async_remote_copy(
        src_ref=src, dst_ref=dst, send_sem=send, recv_sem=recv, device_id=device, device_id_type=MESH
    )


def signal(device):
    pl.semaphore_signal(pltpu.get_barrier_semaphore(), inc=1, device_id=device, device_id_type=MESH)


def block_rows(seen, tokens):
    at = lax.broadcasted_iota(jnp.int32, (PAIR, tokens), 0)
    of = lax.broadcasted_iota(jnp.int32, (PAIR, tokens), 1) // BLK
    return dot_nn(seen, jnp.where(at == of, 1.0, 0.0).astype(BF16))


def spread(rows, count):
    return jnp.concatenate(
        [jnp.broadcast_to(rows[b : b + 1], (BLK, rows.shape[1])) for b in range(count)], axis=0
    )


def layer_kernel(
    nf,
    nz,
    hidden_ref,
    w_ref,
    vecs_ref,
    freq_ref,
    time_ref,
    cond_ref,
    noise_ref,
    blocks_ref,
    counts_ref,
    grad_out,
    d_hidden_out,
    nbuf,
    nt,
    wbuf,
    hbuf,
    qbuf,
    cols,
    base,
    bias,
    bias_t,
    attn,
    stats,
    mbuf,
    rbuf,
    dattn,
    dqkv,
    acc,
    y_buf,
    y_got,
    z_buf,
    z_got,
    res,
    dn_acc,
    dn_buf,
    dn_got,
    w_send,
    w_recv,
    w_own,
    n_send,
    n_recv,
    h_send,
    h_recv,
    m_send,
    m_recv,
    r_send,
    r_recv,
    y_send,
    y_recv,
    z_send,
    z_recv,
    g_send,
    g_recv,
    d_send,
    d_recv,
    o_sem,
):
    me = Place()
    tokens, width = hidden_ref.shape
    gw = width // GROUP
    w_rows = w_ref.shape[0]
    total = GROUP * tokens
    window = 3 * tokens
    local = tokens // BLK
    rows = width // nf
    rc = rows // SPLIT
    per_pair = 3 * SPLIT
    chunks = PAIRS * per_pair
    last = GROUP - 1
    slot = me.g + 1
    lane = lax.broadcasted_iota(jnp.int32, (1, PAIR), 1)
    low = lane < HD

    first_g = me.g == 0
    last_g = me.g == last
    at_edge = jnp.logical_or(first_g, last_g)
    up_z = (me.z + 1) % nz
    down_z = (me.z + nz - 1) % nz
    f_peers = [me.at(f=(me.f + o) % nf) for o in range(1, nf)]
    g_peers = [me.at(g=(me.g + o) % GROUP) for o in range(1, GROUP)]
    to_x = me.at(g=me.g_x)
    to_core = me.at(g=me.g_core)
    halo_x = [me.at(z=jnp.where(me.core == 1, down_z, up_z), g=jnp.where(me.core == 1, last, 0))]
    for device in f_peers + g_peers + [me.at(z=up_z), me.at(z=down_z)] + halo_x:
        signal(device)
    greeted = nf - 1 + GROUP - 1 + 2

    pad = jnp.zeros((5, tokens), F32)
    small = jnp.concatenate([time_ref[...].astype(F32), cond_ref[...].astype(F32), noise_ref[...], pad], axis=0)
    cols[...] = jnp.concatenate([small] + [jnp.zeros((PAIR - 8, tokens), F32)], axis=0).T
    step = 32
    cvec = vecs_ref[0:1, :]
    head = vecs_ref[1:2, :]

    def token_tile(i, carry):
        at = pl.ds(pl.multiple_of(i * step, step), step)
        angle = cols[at, 0:1] * freq_ref[...]
        feats = jnp.concatenate([jnp.sin(angle), jnp.cos(angle)], axis=1)
        h_in = hidden_ref[at, :].astype(F32) + cols[at, 1:2] * cvec + feats
        inv = lax.rsqrt(jnp.mean(h_in * h_in, axis=1, keepdims=True) + EPS)
        hbuf[at, :] = h_in
        nbuf[slot, at, :] = (h_in * inv).astype(BF16)
        base[at, :] = jnp.broadcast_to(jnp.sum(h_in * head, axis=1, keepdims=True), (step, PAIR))
        return carry

    half_tiles = tokens // step // 2
    lax.fori_loop(0, half_tiles, token_tile, 0)

    @pl.when(at_edge)
    def _():
        pl.semaphore_wait(pltpu.get_barrier_semaphore(), greeted + 2)

    @pl.when(jnp.logical_not(at_edge))
    def _():
        pl.semaphore_wait(pltpu.get_barrier_semaphore(), greeted)

    own_rows = pl.ds(pl.multiple_of(me.f * w_rows, w_rows), w_rows)

    def w_part(at):
        p, j = at // 3, at % 3
        col = pl.multiple_of(j * width + me.g * gw + p * PAIR, PAIR)
        return w_ref.at[:, pl.ds(col, PAIR)], wbuf.at[own_rows, at * PAIR : (at + 1) * PAIR]

    def w_copy(at, o):
        src, dst = w_part(at)
        return remote(src, dst, w_send.at[o - 1, at], w_recv.at[o - 1, at], f_peers[o - 1])

    def w_own_copy(at):
        src, dst = w_part(at)
        return pltpu.make_async_copy(src, dst, w_own.at[at])

    for at in range(3 * PAIRS):
        for o in range(1, nf):
            w_copy(at, o).start()

    part_rows = tokens // 2

    def token_copy(slot_at, part, way, to):
        at = slice(0, part_rows) if part == 0 else slice(part_rows, tokens + 16)
        return remote(
            nbuf.at[slot_at, at, :], nbuf.at[slot_at, at, :], n_send.at[way, part], n_recv.at[way, part], to
        )

    token_copy(slot, 0, 0, to_x).start()
    token_copy(slot, 0, 1, to_core).start()
    for at in range(3 * PAIRS):
        w_own_copy(at).start()
    lax.fori_loop(half_tiles, 2 * half_tiles, token_tile, 0)

    at_row = lax.broadcasted_iota(jnp.int32, (16, PAIR), 0)
    at_lane = lax.broadcasted_iota(jnp.int32, (16, PAIR), 1)
    seen = jnp.zeros((16, PAIR), F32)
    seen_t = jnp.zeros((16, PAIR), F32)
    all_blocks = nz * GROUP * local
    for b in range(local):
        for j in range(blocks_ref.shape[2]):
            place = blocks_ref[0, b, j] - (me.seq - 1) * local
            place = jnp.where(place < 0, place + all_blocks, place)
            place = jnp.where(place >= all_blocks, place - all_blocks, place)
            place = jnp.where(j <= counts_ref[0, b], place, -1)
            seen = jnp.where(jnp.logical_and(at_row == b, at_lane == place), 1.0, seen)
            seen_t = jnp.where(jnp.logical_and(at_row == place, at_lane == b), 1.0, seen_t)
    nbuf[slot, tokens:, :PAIR] = seen.astype(BF16)
    nbuf[slot, tokens:, PAIR : 2 * PAIR] = seen_t.astype(BF16)
    nbuf[slot, tokens:, 2 * PAIR :] = jnp.zeros((16, width - 2 * PAIR), BF16)

    token_copy(slot, 1, 0, to_x).start()
    token_copy(slot, 1, 1, to_core).start()

    def halo_copies(dst, z, core):
        return [
            remote(nbuf.at[slot], nbuf.at[dst], h_send.at[x], h_recv.at[0], me.at(z=z, g=2 * x + core))
            for x in range(2)
        ]

    @pl.when(last_g)
    def _():
        for copy in halo_copies(0, up_z, 1):
            copy.start()

    @pl.when(first_g)
    def _():
        for copy in halo_copies(SLOTS - 1, down_z, 0):
            copy.start()

    base_row = base[...].T[0:1, :]

    def turn(slot_at):
        at = pl.ds(pl.multiple_of((slot_at - 1) * tokens, tokens), tokens)
        nt[:, at] = nbuf[slot_at, :tokens, :].T

    def project(slot_at):
        qbuf[slot_at] = dot_nn(nbuf[slot_at, :tokens, :], wbuf[...]).astype(BF16)

    core_slot = me.g_core + 1
    x_slot = me.g_x + 1
    far_slot = me.g_far + 1
    turn(slot)
    for part in range(2):
        token_copy(core_slot, part, 1, to_core).wait_recv()
    turn(core_slot)
    token_copy(x_slot, 0, 0, to_x).wait_recv()
    token_copy(x_slot, 0, 2, to_core).start()
    for at in range(3 * PAIRS):
        w_own_copy(at).wait()
        for o in range(1, nf):
            w_copy(at, o).wait_recv()
    project(slot)
    project(core_slot)
    token_copy(x_slot, 1, 0, to_x).wait_recv()
    token_copy(x_slot, 1, 2, to_core).start()
    project(x_slot)
    turn(x_slot)
    for part in range(2):
        token_copy(far_slot, part, 2, to_core).wait_recv()
    project(far_slot)
    turn(far_slot)

    def fill_bias(c):
        visible = block_rows(nbuf[c + 1, tokens:, :PAIR], window)
        bias[c] = jnp.where(visible[:8] > 0.5, 0.0, NEG)

    def fill_bias_t(c):
        parts = []
        for s in range(3):
            from_slot = block_rows(nbuf[c + s, tokens:, PAIR : 2 * PAIR], tokens)
            parts.append(from_slot[(2 - s) * local : (3 - s) * local])
        visible = jnp.concatenate(parts, axis=1)
        bias_t[c, :local, :] = jnp.where(visible > 0.5, 0.0, NEG)

    for c in range(GROUP):
        fill_bias(c)

    head_group = vecs_ref[1:2, pl.ds(pl.multiple_of(me.g * gw, gw), gw)]
    head_rows = jnp.broadcast_to(head_group, (16, gw)).astype(BF16)

    def forward(c):
        hide = bias[c]
        net = jnp.zeros((16, tokens), F32)
        found = jnp.zeros((tokens, PAIR), F32)
        for p in range(PAIRS):
            q_part = slice(p * TRIO, p * TRIO + PAIR)
            k_part = slice(p * TRIO + PAIR, p * TRIO + 2 * PAIR)
            v_part = slice(p * TRIO + 2 * PAIR, (p + 1) * TRIO)
            query = qbuf[c + 1, :, q_part] * jnp.asarray(SCALE, BF16)
            keys = qbuf[pl.ds(c, 3), :, k_part].reshape(window, PAIR)
            vals = qbuf[pl.ds(c, 3), :, v_part].reshape(window, PAIR)
            outs = []
            for half in range(2):
                mine = low if half == 0 else jnp.logical_not(low)
                scores = dot_nt(jnp.where(mine, query, jnp.zeros_like(query)), keys) + spread(hide, local)
                top = jnp.max(scores, axis=1, keepdims=True)
                expo = jnp.exp(scores - top)
                norm = jnp.sum(expo, axis=1, keepdims=True)
                probs_b = (expo * (1.0 / norm)).astype(BF16)
                outs.append(dot_nn(probs_b, vals))
                found = jnp.where(lane == 2 * p + half, top + jnp.log(norm), found)
            value = jnp.where(low, outs[0], outs[1]).astype(BF16)
            attn[c, :, p * PAIR : (p + 1) * PAIR] = value
            net = net + dot_nt(head_rows[:, p * PAIR : (p + 1) * PAIR], value)
        stats[c] = found
        mbuf[0, c] = net[:8]

    def inner_chunk(i, carry):
        forward(i)
        return carry

    lax.fori_loop(1, GROUP - 1, inner_chunk, 0)

    near_halo = jnp.where(me.core == 1, 0, SLOTS - 1)
    other_halo = jnp.where(me.core == 1, SLOTS - 1, 0)

    def halo_forward(slot_at):
        return remote(nbuf.at[slot_at], nbuf.at[slot_at], h_send.at[2], h_recv.at[1], to_core)

    remote(nbuf.at[near_halo], nbuf.at[near_halo], h_send.at[0], h_recv.at[0], to_x).wait_recv()
    halo_forward(near_halo).start()
    project(near_halo)
    halo_forward(other_halo).wait_recv()
    project(other_halo)

    def outer_chunk(i, carry):
        forward(i * (GROUP - 1))
        return carry

    lax.fori_loop(0, 2, outer_chunk, 0)

    in_row = lax.broadcasted_iota(jnp.int32, (8, tokens), 0)
    for c in range(GROUP):
        mbuf[0, c] = jnp.where(in_row == 0, mbuf[0, c], 0.0)
    extra = jnp.where(
        in_row == 0, base_row + noise_ref[...], jnp.where(in_row == 1, 2.0 * (1.0 - small[1:2, :]), 0.0)
    )
    mbuf[0, me.g] = mbuf[0, me.g] + extra

    def net_copy(o):
        return remote(mbuf.at[0], mbuf.at[o], m_send.at[o - 1], m_recv.at[o - 1], g_peers[o - 1])

    for o in range(1, GROUP):
        net_copy(o).start()
    for c in range(GROUP):
        fill_bias_t(c)
    for o in range(1, GROUP):
        net_copy(o).wait_recv()

    def d_attn_parts(row):
        col = jnp.broadcast_to(row, (PAIR, tokens)).T
        return col, [(col * head_group[:, p * PAIR : (p + 1) * PAIR]).astype(BF16) for p in range(PAIRS)]

    def finish_stats(c):
        msg = mbuf[0, c] + mbuf[1, c] + mbuf[2, c] + mbuf[3, c]
        col, parts = d_attn_parts(msg[0:1] * msg[1:2])
        full = jnp.where(lane == 8, col, stats[c])
        for p, value in enumerate(parts):
            dattn[c + 1, :, p * PAIR : (p + 1) * PAIR] = value
            prod = value.astype(F32) * attn[c, :, p * PAIR : (p + 1) * PAIR].astype(F32)
            sum_low = jnp.sum(jnp.where(low, prod, 0.0), axis=1, keepdims=True)
            sum_high = jnp.sum(jnp.where(low, 0.0, prod), axis=1, keepdims=True)
            full = jnp.where(lane == 4 + 2 * p, sum_low, full)
            full = jnp.where(lane == 5 + 2 * p, sum_high, full)
        stats[c] = full
        rbuf[c + 1] = full.T[:16, :]

    up_copy = remote(rbuf.at[GROUP], rbuf.at[0], r_send.at[0], r_recv.at[0], me.at(z=up_z))
    down_copy = remote(rbuf.at[1], rbuf.at[SLOTS - 1], r_send.at[1], r_recv.at[1], me.at(z=down_z))
    finish_stats(0)
    down_copy.start()
    finish_stats(GROUP - 1)
    up_copy.start()
    for c in range(1, GROUP - 1):
        finish_stats(c)

    def backward(c, p):
        q_part = slice(p * TRIO, p * TRIO + PAIR)
        k_part = slice(p * TRIO + PAIR, p * TRIO + 2 * PAIR)
        v_part = slice(p * TRIO + 2 * PAIR, (p + 1) * TRIO)
        a_part = slice(p * PAIR, (p + 1) * PAIR)
        hide = bias[c]
        hide_t = bias_t[c]
        found = stats[c]
        scale = jnp.asarray(SCALE, BF16)
        query = qbuf[pl.ds(c, 3), :, q_part].reshape(window, PAIR) * scale
        own_query = qbuf[c + 1, :, q_part] * scale
        keys = qbuf[pl.ds(c, 3), :, k_part].reshape(window, PAIR)
        vals = qbuf[pl.ds(c, 3), :, v_part].reshape(window, PAIR)
        own_keys = qbuf[c + 1, :, k_part]
        own_vals = qbuf[c + 1, :, v_part]
        d_attn = dattn[pl.ds(c, 3), :, a_part].reshape(window, PAIR)
        own_d_attn = dattn[c + 1, :, a_part]
        rows_of = [rbuf[c + s] for s in range(3)]
        d_q, d_k, d_v = [], [], []
        for half in range(2):
            mine = low if half == 0 else jnp.logical_not(low)
            h = 2 * p + half
            lse = found[:, h : h + 1]
            delta = found[:, 4 + h : 5 + h]
            probs = jnp.exp(
                dot_nt(jnp.where(mine, own_query, jnp.zeros_like(own_query)), keys) + spread(hide, local) - lse
            )
            d_probs = dot_nt(jnp.where(mine, own_d_attn, jnp.zeros_like(own_d_attn)), vals)
            d_scores = (probs * (d_probs - delta)).astype(BF16)
            d_q.append(dot_nn(d_scores, keys))
            lse_row = jnp.concatenate([r[h : h + 1] for r in rows_of], axis=1)
            delta_row = jnp.concatenate([r[4 + h : 5 + h] for r in rows_of], axis=1)
            own_keys_m = jnp.where(mine, own_keys, jnp.zeros_like(own_keys))
            own_vals_m = jnp.where(mine, own_vals, jnp.zeros_like(own_vals))
            probs_t = jnp.exp(dot_nt(own_keys_m, query) + spread(hide_t, local) - lse_row)
            d_v.append(dot_nn(probs_t.astype(BF16), d_attn))
            d_probs_t = dot_nt(own_vals_m, d_attn)
            d_scores_t = (probs_t * (d_probs_t - delta_row)).astype(BF16)
            d_k.append(dot_nn(d_scores_t, query))
        at = pl.ds(pl.multiple_of(c * tokens, tokens), tokens) if not isinstance(c, int) else slice(
            c * tokens, (c + 1) * tokens
        )
        dqkv[at, p * TRIO : p * TRIO + PAIR] = (jnp.where(low, d_q[0], d_q[1]) * SCALE).astype(BF16)
        dqkv[at, p * TRIO + PAIR : p * TRIO + 2 * PAIR] = jnp.where(low, d_k[0], d_k[1]).astype(BF16)
        dqkv[at, p * TRIO + 2 * PAIR : (p + 1) * TRIO] = jnp.where(low, d_v[0], d_v[1]).astype(BF16)

    def y_copy(o, k):
        return remote(
            y_buf.at[o - 1, k], y_got.at[o - 1, k], y_send.at[o - 1, k], y_recv.at[o - 1, k], f_peers[o - 1]
        )

    def product(f, p):
        at = pl.ds(pl.multiple_of(f * rows, rows), rows)
        return dot_nn(nt[at, :], dqkv[:, p * TRIO : (p + 1) * TRIO])

    def pieces(p):
        for j in range(3):
            for r in range(SPLIT):
                yield (p * 3 + j) * SPLIT + r, slice(r * rc, (r + 1) * rc), slice(j * PAIR, (j + 1) * PAIR)

    def send_grads(p):
        for o in range(1, nf):
            part = product((me.f + o) % nf, p).astype(BF16)
            for k, r_at, c_at in pieces(p):
                y_buf[o - 1, k] = part[r_at, c_at]
                y_copy(o, k).start()

    def keep_grads(p):
        part = product(me.f, p)
        for k, r_at, c_at in pieces(p):
            acc[k] = part[r_at, c_at]

    lower = me.z < nz // 2
    depth = jnp.where(lower, me.z, nz - 1 - me.z)
    outer = depth == 0
    has_outer = jnp.logical_not(outer)
    inner = depth == nz // 2 - 1
    not_inner = jnp.logical_not(inner)
    inward = me.at(z=jnp.where(lower, up_z, down_z))
    outward = me.at(z=jnp.where(lower, down_z, up_z))

    def z_copy(k, way):
        return remote(z_buf.at[k], z_got.at[way, k], z_send.at[0, k], z_recv.at[way, k], inward)

    def result_copy(k):
        ref = res.at[me.g, k]
        return remote(ref, ref, z_send.at[1, k], z_recv.at[2, k], outward)

    def g_copy(g, k, way, to):
        return remote(res.at[g, k], res.at[g, k], g_send.at[way, k], g_recv.at[way, k], to)

    def out_copy(g, k):
        p, j, r = k // per_pair, k // SPLIT % 3, k % SPLIT
        at = pl.ds(pl.multiple_of(j * width + g * gw + p * PAIR, PAIR), PAIR)
        return pltpu.make_async_copy(res.at[g, k], grad_out.at[r * rc : (r + 1) * rc, at], o_sem.at[g, k])

    def stage_a(k):
        value = acc[k]
        for o in range(1, nf):
            y_copy(o, k).wait_recv()
            value = value + y_got[o - 1, k].astype(F32)
        acc[k] = value

        @pl.when(outer)
        def _():
            z_buf[k] = acc[k].astype(BF16)
            z_copy(k, 0).start()

    def stage_b(k):
        @pl.when(has_outer)
        def _():
            z_copy(k, 0).wait_recv()
            z_buf[k] = (acc[k] + z_got[0, k].astype(F32)).astype(BF16)

            @pl.when(inner)
            def _():
                z_copy(k, 1).start()

            @pl.when(not_inner)
            def _():
                z_copy(k, 0).start()

    def stage_c(k):
        @pl.when(inner)
        def _():
            z_copy(k, 1).wait_recv()
            res[me.g, k] = (z_buf[k].astype(F32) + z_got[1, k].astype(F32)).astype(BF16)

        @pl.when(not_inner)
        def _():
            result_copy(k).wait_recv()

        @pl.when(has_outer)
        def _():
            result_copy(k).start()

        g_copy(me.g, k, 0, to_x).start()
        g_copy(me.g, k, 1, to_core).start()
        out_copy(me.g, k).start()

    def stage_d(k):
        g_copy(me.g_x, k, 0, to_x).wait_recv()
        g_copy(me.g_x, k, 2, to_core).start()
        out_copy(me.g_x, k).start()

    def stage_e(k):
        g_copy(me.g_core, k, 1, to_core).wait_recv()
        out_copy(me.g_core, k).start()
        g_copy(me.g_far, k, 2, to_core).wait_recv()
        out_copy(me.g_far, k).start()

    def inner_backward(i, carry):
        backward(i, 0)
        return carry

    lax.fori_loop(1, GROUP - 1, inner_backward, 0)
    up_copy.wait_recv()
    down_copy.wait_recv()
    for j in (0, SLOTS - 1):
        unused, parts = d_attn_parts(rbuf[j][8:9, :])
        for p, value in enumerate(parts):
            dattn[j, :, p * PAIR : (p + 1) * PAIR] = value

    def outer_backward(i, carry):
        backward(i * (GROUP - 1), 0)
        return carry

    lax.fori_loop(0, 2, outer_backward, 0)
    send_grads(0)
    keep_grads(0)
    backward(0, 1)
    backward(1, 1)
    for k in range(0, 4):
        stage_a(k)
    backward(2, 1)
    for k in range(4, 6):
        stage_a(k)
    for k in range(0, 4):
        stage_b(k)
    backward(3, 1)
    send_grads(1)
    for k in range(4, 6):
        stage_b(k)
    for k in range(0, 4):
        stage_c(k)

    def d_normed(g):
        at = pl.ds(pl.multiple_of(g * tokens, tokens), tokens)
        return dot_nt(dqkv[at, :], wbuf[...])

    def d_copy(at):
        to = to_x if at == 2 else to_core
        return remote(dn_buf.at[at], dn_got.at[at], d_send.at[at], d_recv.at[at], to)

    dn_buf[0] = d_normed(me.g_far).astype(BF16)
    d_copy(0).start()
    dn_buf[1] = d_normed(me.g_core).astype(BF16)
    d_copy(1).start()
    keep_grads(1)
    dn_x = d_normed(me.g_x)
    d_copy(0).wait_recv()
    dn_buf[2] = (dn_x + dn_got[0].astype(F32)).astype(BF16)
    d_copy(2).start()
    dn_acc[...] = d_normed(me.g)

    def d_hidden():
        d_copy(1).wait_recv()
        d_copy(2).wait_recv()

        def tile(i, carry):
            at = pl.ds(pl.multiple_of(i * step, step), step)
            d_norm = dn_acc[at, :] + dn_got[1, at, :].astype(F32) + dn_got[2, at, :].astype(F32)
            h_in = hbuf[at, :]
            inv = lax.rsqrt(jnp.mean(h_in * h_in, axis=1, keepdims=True) + EPS)
            d_out = stats[me.g, at, 8:9] * head
            mean = jnp.mean(d_norm * h_in, axis=1, keepdims=True)
            d_hidden_out[at, :] = (d_out + inv * (d_norm - h_in * inv * inv * mean)).astype(BF16)
            return carry

        lax.fori_loop(0, tokens // step, tile, 0)

    stages = (stage_a, stage_b, stage_c, stage_d, stage_e)
    done = [per_pair, per_pair, 4, 0, 0]
    order = []
    for t in range(chunks + len(stages)):
        for at, stage in enumerate(stages):
            goal = min(chunks, per_pair + t - at + 1) if at < 2 else min(chunks, per_pair + t - at)
            while done[at] < goal and (at == 0 or done[at] < done[at - 1]):
                stage(done[at])
                done[at] += 1
        if t == per_pair - 1:
            d_hidden()
    for at, stage in enumerate(stages):
        for k in range(done[at], chunks):
            stage(k)

    for at in range(3 * PAIRS):
        for o in range(1, nf):
            w_copy(at, o).wait_send()
    for part in range(2):
        for way, to in ((0, to_x), (1, to_core)):
            token_copy(slot, part, way, to).wait_send()
        token_copy(x_slot, part, 2, to_core).wait_send()
    halo_forward(near_halo).wait_send()

    @pl.when(last_g)
    def _():
        for copy in halo_copies(0, up_z, 1):
            copy.wait_send()

    @pl.when(first_g)
    def _():
        for copy in halo_copies(SLOTS - 1, down_z, 0):
            copy.wait_send()

    for o in range(1, GROUP):
        net_copy(o).wait_send()
    up_copy.wait_send()
    down_copy.wait_send()
    for at in range(3):
        d_copy(at).wait_send()
    for k in range(chunks):
        for o in range(1, nf):
            y_copy(o, k).wait_send()
        z_copy(k, 0).wait_send()
        g_copy(me.g, k, 0, to_x).wait_send()
        g_copy(me.g, k, 1, to_core).wait_send()
        g_copy(me.g_x, k, 2, to_core).wait_send()
        for g in (me.g, me.g_x, me.g_core, me.g_far):
            out_copy(g, k).wait()

    @pl.when(has_outer)
    def _():
        for k in range(chunks):
            result_copy(k).wait_send()


def layer_call(nf, nz, hidden, w, vecs, freq, time_idx, cond_mask, noise, blocks, counts):
    tokens, width = hidden.shape
    rows = width // nf
    rc = rows // SPLIT
    chunks = PAIRS * 3 * SPLIT
    gw = width // GROUP
    dma = pltpu.SemaphoreType.DMA
    return pl.pallas_call(
        functools.partial(layer_kernel, nf, nz),
        in_specs=[VMEM, ANY, VMEM, VMEM, VMEM, VMEM, VMEM, SMEM, SMEM],
        out_specs=[ANY, VMEM],
        out_shape=[
            jax.ShapeDtypeStruct((rows, 3 * width), BF16),
            jax.ShapeDtypeStruct((tokens, width), BF16),
        ],
        scratch_shapes=[
            pltpu.VMEM((SLOTS, tokens + 16, width), BF16),
            pltpu.VMEM((width, GROUP * tokens), BF16),
            pltpu.VMEM((width, 3 * gw), BF16),
            pltpu.VMEM((tokens, width), F32),
            pltpu.VMEM((SLOTS, tokens, 3 * gw), BF16),
            pltpu.VMEM((tokens, PAIR), F32),
            pltpu.VMEM((tokens, PAIR), F32),
            pltpu.VMEM((GROUP, 8, 3 * tokens), F32),
            pltpu.VMEM((GROUP, 8, 3 * tokens), F32),
            pltpu.VMEM((GROUP, tokens, gw), BF16),
            pltpu.VMEM((GROUP, tokens, PAIR), F32),
            pltpu.VMEM((GROUP, GROUP, 8, tokens), F32),
            pltpu.VMEM((SLOTS, 16, tokens), F32),
            pltpu.VMEM((SLOTS, tokens, gw), BF16),
            pltpu.VMEM((GROUP * tokens, 3 * gw), BF16),
            pltpu.VMEM((chunks, rc, PAIR), F32),
            pltpu.VMEM((nf - 1, chunks, rc, PAIR), BF16),
            pltpu.VMEM((nf - 1, chunks, rc, PAIR), BF16),
            pltpu.VMEM((chunks, rc, PAIR), BF16),
            pltpu.VMEM((2, chunks, rc, PAIR), BF16),
            pltpu.VMEM((GROUP, chunks, rc, PAIR), BF16),
            pltpu.VMEM((tokens, width), F32),
            pltpu.VMEM((3, tokens, width), BF16),
            pltpu.VMEM((3, tokens, width), BF16),
            dma((nf - 1, 3 * PAIRS)),
            dma((nf - 1, 3 * PAIRS)),
            dma((3 * PAIRS,)),
            dma((3, 2)),
            dma((3, 2)),
            dma((3,)),
            dma((2,)),
            dma((GROUP - 1,)),
            dma((GROUP - 1,)),
            dma((2,)),
            dma((2,)),
            dma((nf - 1, chunks)),
            dma((nf - 1, chunks)),
            dma((2, chunks)),
            dma((3, chunks)),
            dma((3, chunks)),
            dma((3, chunks)),
            dma((3,)),
            dma((3,)),
            dma((GROUP, chunks)),
        ],
        compiler_params=pltpu.CompilerParams(
            collective_id=0, has_side_effects=True, vmem_limit_bytes=56 << 20
        ),
        name="layer",
    )(hidden, w, vecs, freq, time_idx, cond_mask, noise, blocks, counts)


def body(hidden, w_qkv, cond_vec, head_w, blocks, counts, time_idx, cond_mask, noise):
    width = hidden.shape[2]
    half = width // 2
    nf = lax.axis_size("fsdp")
    nz = lax.axis_size("seq") // GROUP
    freq = np.exp(np.float32(-math.log(10000.0)) * np.arange(half, dtype=np.float32) / np.float32(half))
    vecs = jnp.stack([cond_vec, head_w]).astype(F32)
    grad, d_hidden = layer_call(
        nf,
        nz,
        hidden[0],
        w_qkv,
        vecs,
        jnp.asarray(freq.astype(np.float32))[None, :],
        time_idx,
        cond_mask,
        noise,
        blocks,
        counts,
    )
    return (d_hidden[None], grad.astype(F32))


def solution(mesh):
    return jax.shard_map(
        body,
        mesh=mesh,
        in_specs=(
            P("fsdp", "seq", None),
            P("fsdp", None),
            P(),
            P(),
            P("fsdp", "seq", None),
            P("fsdp", "seq"),
            P("fsdp", "seq"),
            P("fsdp", "seq"),
            P("fsdp", "seq"),
        ),
        out_specs=(P("fsdp", "seq", None), P("fsdp", None)),
        check_vma=False,
    )
```

```python
import functools
import math

import jax
import jax.numpy as jnp
import numpy as np
from jax import lax
from jax.experimental import pallas as pl
from jax.experimental.pallas import tpu as pltpu
from jax.sharding import PartitionSpec as P

HD = 64
BLK = 64
PAIR = 2 * HD
TRIO = 3 * PAIR
GROUP = 4
PAIRS = 2
SLOTS = GROUP + 2
SPLIT = 2
LAG_B = 3
LAG_C = 7
EPS = 1e-05
SCALE = HD ** (-0.5)
NEG = -1e30
F32 = jnp.float32
BF16 = jnp.bfloat16
MESH = pl.DeviceIdType.MESH
ANY = pl.BlockSpec(memory_space=pl.ANY)
HBM = pl.BlockSpec(memory_space=pltpu.HBM)
VMEM = pl.BlockSpec(memory_space=pltpu.VMEM)
SMEM = pl.BlockSpec(memory_space=pltpu.SMEM)


def dot_nt(a, b):
    return lax.dot_general(a, b, (((1,), (1,)), ((), ())), preferred_element_type=F32)


def dot_nn(a, b):
    return jnp.dot(a, b, preferred_element_type=F32)


class Place:
    def __init__(self):
        seq = lax.axis_index("seq")
        self.seq = seq
        self.f = lax.axis_index("fsdp")
        self.z = seq // GROUP
        self.g = seq % GROUP
        self.core = self.g % 2
        self.x = self.g // 2
        self.g_core = self.x * 2 + 1 - self.core
        self.g_x = (1 - self.x) * 2 + self.core
        self.g_far = (1 - self.x) * 2 + 1 - self.core

    def at(self, z=None, g=None, f=None):
        z = self.z if z is None else z
        g = self.g if g is None else g
        f = self.f if f is None else f
        return (z * GROUP + g, f)


def remote(src, dst, send, recv, device):
    return pltpu.make_async_remote_copy(
        src_ref=src, dst_ref=dst, send_sem=send, recv_sem=recv, device_id=device, device_id_type=MESH
    )


def signal(device):
    pl.semaphore_signal(pltpu.get_barrier_semaphore(), inc=1, device_id=device, device_id_type=MESH)


def one_row(ref):
    value = ref[...].astype(F32)
    return jnp.concatenate([value[i : i + 1] for i in range(value.shape[0])], axis=1)


def block_rows(seen, tokens):
    at = lax.broadcasted_iota(jnp.int32, (PAIR, tokens), 0)
    of = lax.broadcasted_iota(jnp.int32, (PAIR, tokens), 1) // BLK
    return dot_nn(seen, jnp.where(at == of, 1.0, 0.0).astype(BF16))


def spread(rows, count):
    return jnp.concatenate(
        [jnp.broadcast_to(rows[b : b + 1], (BLK, rows.shape[1])) for b in range(count)], axis=0
    )


def layer_kernel(
    nf,
    nz,
    hidden_hbm,
    w_ref,
    cvec_hbm,
    head_hbm,
    freq_hbm,
    time_hbm,
    cond_hbm,
    noise_hbm,
    blocks_hbm,
    counts_hbm,
    grad_out,
    d_hidden_out,
    hidden_ref,
    cvec_ref,
    head_ref,
    freq_ref,
    time_ref,
    cond_ref,
    noise_ref,
    blocks_ref,
    counts_ref,
    head_row,
    nbuf,
    nt,
    wbuf,
    hbuf,
    qbuf,
    cols,
    base,
    bias,
    bias_t,
    attn,
    stats,
    mbuf,
    rbuf,
    dattn,
    dqkv,
    acc,
    y_buf,
    y_got,
    z_buf,
    z_got,
    res,
    dn_acc,
    dn_buf,
    dn_got,
    w_send,
    w_recv,
    w_own,
    n_send,
    n_recv,
    h_send,
    h_recv,
    m_send,
    m_recv,
    r_send,
    r_recv,
    y_send,
    y_recv,
    z_send,
    z_recv,
    g_send,
    g_recv,
    d_send,
    d_recv,
    o_sem,
    in_sem,
):
    me = Place()
    loads = [
        pltpu.make_async_copy(src, dst, in_sem.at[at])
        for at, (src, dst) in enumerate(
            (
                (hidden_hbm, hidden_ref),
                (cvec_hbm, cvec_ref),
                (head_hbm, head_ref),
                (freq_hbm, freq_ref),
                (time_hbm, time_ref),
                (cond_hbm, cond_ref),
                (noise_hbm, noise_ref),
                (blocks_hbm, blocks_ref),
                (counts_hbm, counts_ref),
            )
        )
    ]
    for copy in loads:
        copy.start()
    tokens, width = hidden_ref.shape
    gw = width // GROUP
    w_rows = w_ref.shape[0]
    total = GROUP * tokens
    window = 3 * tokens
    local = tokens // BLK
    rows = width // nf
    rc = rows // SPLIT
    per_pair = 3 * SPLIT
    chunks = PAIRS * per_pair
    slot = me.g + 1
    lane = lax.broadcasted_iota(jnp.int32, (1, PAIR), 1)
    low = lane < HD

    up_z = (me.z + 1) % nz
    down_z = (me.z + nz - 1) % nz
    f_peers = [me.at(f=(me.f + o) % nf) for o in range(1, nf)]
    g_peers = [me.at(g=(me.g + o) % GROUP) for o in range(1, GROUP)]
    to_x = me.at(g=me.g_x)
    to_core = me.at(g=me.g_core)
    for device in f_peers + g_peers + [me.at(z=up_z), me.at(z=down_z)]:
        signal(device)
    greeted = nf - 1 + GROUP - 1 + 2

    for copy in loads:
        copy.wait()

    pad = jnp.zeros((5, tokens), F32)
    small = jnp.concatenate([time_ref[...].astype(F32), cond_ref[...].astype(F32), noise_ref[...], pad], axis=0)
    cols[...] = jnp.concatenate([small] + [jnp.zeros((PAIR - 8, tokens), F32)], axis=0).T
    step = 32
    cvec = one_row(cvec_ref)
    head_row[...] = one_row(head_ref)
    head = head_row[...]

    def token_tile(i, carry):
        at = pl.ds(pl.multiple_of(i * step, step), step)
        angle = cols[at, 0:1] * freq_ref[...]
        feats = jnp.concatenate([jnp.sin(angle), jnp.cos(angle)], axis=1)
        h_in = hidden_ref[at, :].astype(F32) + cols[at, 1:2] * cvec + feats
        inv = lax.rsqrt(jnp.mean(h_in * h_in, axis=1, keepdims=True) + EPS)
        hbuf[at, :] = h_in
        nbuf[slot, at, :] = (h_in * inv).astype(BF16)
        base[at, :] = jnp.broadcast_to(jnp.sum(h_in * head, axis=1, keepdims=True), (step, PAIR))
        return carry

    half_tiles = tokens // step // 2
    lax.fori_loop(0, half_tiles, token_tile, 0)

    pl.semaphore_wait(pltpu.get_barrier_semaphore(), greeted)

    odd = me.z % 2
    fetched = [odd * 4, odd * 4 + 1, 2, 3]
    passed = [4 - odd * 4, 5 - odd * 4]
    z_mate = me.at(z=me.z + 1 - 2 * odd)

    def w_piece(at):
        col = pl.multiple_of(at % 3 * width + me.g * gw + at // 3 * PAIR, PAIR)
        return w_ref.at[:, pl.ds(col, PAIR)]

    def w_place(f, at):
        f_rows = pl.ds(pl.multiple_of(f * w_rows, w_rows), w_rows)
        return wbuf.at[f_rows, pl.ds(pl.multiple_of(at * PAIR, PAIR), PAIR)]

    def w_copy(i, o):
        at = fetched[i]
        return remote(w_piece(at), w_place(me.f, at), w_send.at[o - 1, i], w_recv.at[o - 1, i], f_peers[o - 1])

    def w_got_copy(i, o):
        ref = w_place((me.f + nf - o) % nf, fetched[i])
        return remote(ref, ref, w_send.at[o - 1, i], w_recv.at[o - 1, i], f_peers[o - 1])

    def w_pass_copy(i, o):
        ref = w_place((me.f + nf - o) % nf, fetched[i])
        return remote(ref, ref, w_send.at[o - 1, 4 + i], w_recv.at[o - 1, 4 + i], z_mate)

    def w_passed_copy(i, o):
        ref = w_place((me.f + nf - o) % nf, passed[i])
        return remote(ref, ref, w_send.at[o - 1, 4 + i], w_recv.at[o - 1, 4 + i], z_mate)

    def w_own_copy(at):
        return pltpu.make_async_copy(w_piece(at), w_place(me.f, at), w_own.at[at])

    for i in range(4):
        for o in range(1, nf):
            w_copy(i, o).start()

    part_rows = tokens // 2

    def token_copy(slot_at, part, way, to):
        at = slice(0, part_rows) if part == 0 else slice(part_rows, tokens + 16)
        return remote(
            nbuf.at[slot_at, at, :], nbuf.at[slot_at, at, :], n_send.at[way, part], n_recv.at[way, part], to
        )

    token_copy(slot, 0, 0, to_x).start()
    token_copy(slot, 0, 1, to_core).start()
    for at in range(3 * PAIRS):
        w_own_copy(at).start()
    lax.fori_loop(half_tiles, 2 * half_tiles, token_tile, 0)

    at_row = lax.broadcasted_iota(jnp.int32, (16, PAIR), 0)
    at_lane = lax.broadcasted_iota(jnp.int32, (16, PAIR), 1)
    seen = jnp.zeros((16, PAIR), F32)
    seen_t = jnp.zeros((16, PAIR), F32)
    all_blocks = nz * GROUP * local
    for b in range(local):
        for j in range(blocks_ref.shape[2]):
            place = blocks_ref[0, b, j] - (me.seq - 1) * local
            place = jnp.where(place < 0, place + all_blocks, place)
            place = jnp.where(place >= all_blocks, place - all_blocks, place)
            place = jnp.where(j <= counts_ref[0, b], place, -1)
            seen = jnp.where(jnp.logical_and(at_row == b, at_lane == place), 1.0, seen)
            seen_t = jnp.where(jnp.logical_and(at_row == place, at_lane == b), 1.0, seen_t)
    nbuf[slot, tokens:, :PAIR] = seen.astype(BF16)
    nbuf[slot, tokens:, PAIR : 2 * PAIR] = seen_t.astype(BF16)
    nbuf[slot, tokens:, 2 * PAIR :] = jnp.zeros((16, width - 2 * PAIR), BF16)

    token_copy(slot, 1, 0, to_x).start()
    token_copy(slot, 1, 1, to_core).start()

    upward = me.core == 1
    halo_slot = jnp.where(upward, GROUP, 1)
    near_halo = jnp.where(upward, 0, SLOTS - 1)
    other_halo = jnp.where(upward, SLOTS - 1, 0)
    halo_to = me.at(z=jnp.where(upward, up_z, down_z))

    def part_of(part):
        return slice(0, part_rows) if part == 0 else slice(part_rows, tokens + 16)

    def halo_copy(part):
        at = part_of(part)
        return remote(
            nbuf.at[halo_slot, at, :], nbuf.at[near_halo, at, :], h_send.at[0, part], h_recv.at[0, part], halo_to
        )

    def halo_forward(slot_at, part):
        ref = nbuf.at[slot_at, part_of(part), :]
        return remote(ref, ref, h_send.at[1, part], h_recv.at[1, part], to_core)

    at_end = me.z == jnp.where(upward, nz - 1, 0)
    early_halo = me.x == me.core

    @pl.when(early_halo)
    def _():
        for part in range(2):
            halo_copy(part).start()

    for i in range(2):
        for o in range(1, nf):
            w_got_copy(i, o).wait_recv()
            w_pass_copy(i, o).start()
    base_row = base[...].T[0:1, :]

    def turn(slot_at):
        at = pl.ds(pl.multiple_of((slot_at - 1) * tokens, tokens), tokens)
        nt[:, at] = nbuf[slot_at, :tokens, :].T

    def project(slot_at):
        qbuf[slot_at] = dot_nn(nbuf[slot_at, :tokens, :], wbuf[...]).astype(BF16)

    core_slot = me.g_core + 1
    x_slot = me.g_x + 1
    far_slot = me.g_far + 1
    turn(slot)
    for part in range(2):
        token_copy(core_slot, part, 1, to_core).wait_recv()
    turn(core_slot)
    token_copy(x_slot, 0, 0, to_x).wait_recv()
    token_copy(x_slot, 0, 2, to_core).start()

    for i in range(2):
        for o in range(1, nf):
            w_passed_copy(i, o).wait_recv()
            w_got_copy(2 + i, o).wait_recv()
    for at in range(3 * PAIRS):
        w_own_copy(at).wait()
    project(slot)
    project(core_slot)
    token_copy(x_slot, 1, 0, to_x).wait_recv()
    token_copy(x_slot, 1, 2, to_core).start()

    @pl.when(jnp.logical_not(early_halo))
    def _():
        for part in range(2):
            halo_copy(part).start()

    project(x_slot)
    turn(x_slot)
    for part in range(2):
        token_copy(far_slot, part, 2, to_core).wait_recv()
    project(far_slot)
    turn(far_slot)

    def fill_bias(c):
        visible = block_rows(nbuf[c + 1, tokens:, :PAIR], window)
        bias[c] = jnp.where(visible[:8] > 0.5, 0.0, NEG)

    def fill_bias_t(c):
        parts = []
        for s in range(3):
            from_slot = block_rows(nbuf[c + s, tokens:, PAIR : 2 * PAIR], tokens)
            parts.append(from_slot[(2 - s) * local : (3 - s) * local])
        visible = jnp.concatenate(parts, axis=1)
        bias_t[c, :local, :] = jnp.where(visible > 0.5, 0.0, NEG)

    head_group = head_row[0:1, pl.ds(pl.multiple_of(me.g * gw, gw), gw)]
    head_rows = jnp.broadcast_to(head_group, (16, gw)).astype(BF16)

    def forward(c):
        fill_bias(c)
        hide = bias[c]
        net = jnp.zeros((16, tokens), F32)
        found = jnp.zeros((tokens, PAIR), F32)
        for p in range(PAIRS):
            q_part = slice(p * TRIO, p * TRIO + PAIR)
            k_part = slice(p * TRIO + PAIR, p * TRIO + 2 * PAIR)
            v_part = slice(p * TRIO + 2 * PAIR, (p + 1) * TRIO)
            query = qbuf[c + 1, :, q_part] * jnp.asarray(SCALE, BF16)
            keys = qbuf[pl.ds(c, 3), :, k_part].reshape(window, PAIR)
            vals = qbuf[pl.ds(c, 3), :, v_part].reshape(window, PAIR)
            outs = []
            for half in range(2):
                mine = low if half == 0 else jnp.logical_not(low)
                scores = dot_nt(jnp.where(mine, query, jnp.zeros_like(query)), keys) + spread(hide, local)
                top = jnp.max(scores, axis=1, keepdims=True)
                expo = jnp.exp(scores - top)
                norm = jnp.sum(expo, axis=1, keepdims=True)
                probs_b = (expo * (1.0 / norm)).astype(BF16)
                outs.append(dot_nn(probs_b, vals))
                found = jnp.where(lane == 2 * p + half, top + jnp.log(norm), found)
            value = jnp.where(low, outs[0], outs[1]).astype(BF16)
            attn[c, :, p * PAIR : (p + 1) * PAIR] = value
            net = net + dot_nt(head_rows[:, p * PAIR : (p + 1) * PAIR], value)
        stats[c] = found
        mbuf[0, c] = net[:8]

    def inner_chunk(i, carry):
        forward(i)
        return carry

    lax.fori_loop(1, GROUP - 1, inner_chunk, 0)
    for part in range(2):
        halo_copy(part).wait_recv()
        halo_forward(near_halo, part).start()
    project(near_halo)
    for part in range(2):
        halo_forward(other_halo, part).wait_recv()
    project(other_halo)

    def outer_chunk(i, carry):
        forward(i * (GROUP - 1))
        return carry

    lax.fori_loop(0, 2, outer_chunk, 0)

    in_row = lax.broadcasted_iota(jnp.int32, (8, tokens), 0)
    for c in range(GROUP):
        mbuf[0, c] = jnp.where(in_row == 0, mbuf[0, c], 0.0)
    extra = jnp.where(
        in_row == 0, base_row + noise_ref[...], jnp.where(in_row == 1, 2.0 * (1.0 - small[1:2, :]), 0.0)
    )
    mbuf[0, me.g] = mbuf[0, me.g] + extra

    def net_copy(o):
        return remote(mbuf.at[0], mbuf.at[o], m_send.at[o - 1], m_recv.at[o - 1], g_peers[o - 1])

    for o in range(1, GROUP):
        net_copy(o).start()
    for c in range(GROUP):
        fill_bias_t(c)
    for o in range(1, GROUP):
        net_copy(o).wait_recv()

    def d_attn_parts(row):
        col = jnp.broadcast_to(row, (PAIR, tokens)).T
        return col, [(col * head_group[:, p * PAIR : (p + 1) * PAIR]).astype(BF16) for p in range(PAIRS)]

    def finish_stats(c):
        msg = mbuf[0, c] + mbuf[1, c] + mbuf[2, c] + mbuf[3, c]
        col, parts = d_attn_parts(msg[0:1] * msg[1:2])
        full = jnp.where(lane == 8, col, stats[c])
        for p, value in enumerate(parts):
            dattn[c + 1, :, p * PAIR : (p + 1) * PAIR] = value
            prod = value.astype(F32) * attn[c, :, p * PAIR : (p + 1) * PAIR].astype(F32)
            sum_low = jnp.sum(jnp.where(low, prod, 0.0), axis=1, keepdims=True)
            sum_high = jnp.sum(jnp.where(low, 0.0, prod), axis=1, keepdims=True)
            full = jnp.where(lane == 4 + 2 * p, sum_low, full)
            full = jnp.where(lane == 5 + 2 * p, sum_high, full)
        stats[c] = full
        rbuf[c + 1] = full.T[:16, :]

    up_copy = remote(rbuf.at[GROUP], rbuf.at[0], r_send.at[0], r_recv.at[0], me.at(z=up_z))
    down_copy = remote(rbuf.at[1], rbuf.at[SLOTS - 1], r_send.at[1], r_recv.at[1], me.at(z=down_z))
    finish_stats(0)
    down_copy.start()
    finish_stats(GROUP - 1)
    up_copy.start()
    for c in range(1, GROUP - 1):
        finish_stats(c)

    def backward(c, p):
        q_part = slice(p * TRIO, p * TRIO + PAIR)
        k_part = slice(p * TRIO + PAIR, p * TRIO + 2 * PAIR)
        v_part = slice(p * TRIO + 2 * PAIR, (p + 1) * TRIO)
        a_part = slice(p * PAIR, (p + 1) * PAIR)
        hide = bias[c]
        hide_t = bias_t[c]
        found = stats[c]
        scale = jnp.asarray(SCALE, BF16)
        query = qbuf[pl.ds(c, 3), :, q_part].reshape(window, PAIR) * scale
        own_query = qbuf[c + 1, :, q_part] * scale
        keys = qbuf[pl.ds(c, 3), :, k_part].reshape(window, PAIR)
        vals = qbuf[pl.ds(c, 3), :, v_part].reshape(window, PAIR)
        own_keys = qbuf[c + 1, :, k_part]
        own_vals = qbuf[c + 1, :, v_part]
        d_attn = dattn[pl.ds(c, 3), :, a_part].reshape(window, PAIR)
        own_d_attn = dattn[c + 1, :, a_part]
        rows_of = [rbuf[c + s] for s in range(3)]
        d_q, d_k, d_v = [], [], []
        for half in range(2):
            mine = low if half == 0 else jnp.logical_not(low)
            h = 2 * p + half
            lse = found[:, h : h + 1]
            delta = found[:, 4 + h : 5 + h]
            probs = jnp.exp(
                dot_nt(jnp.where(mine, own_query, jnp.zeros_like(own_query)), keys) + spread(hide, local) - lse
            )
            d_probs = dot_nt(jnp.where(mine, own_d_attn, jnp.zeros_like(own_d_attn)), vals)
            d_scores = (probs * (d_probs - delta)).astype(BF16)
            d_q.append(dot_nn(d_scores, keys))
            lse_row = jnp.concatenate([r[h : h + 1] for r in rows_of], axis=1)
            delta_row = jnp.concatenate([r[4 + h : 5 + h] for r in rows_of], axis=1)
            own_keys_m = jnp.where(mine, own_keys, jnp.zeros_like(own_keys))
            own_vals_m = jnp.where(mine, own_vals, jnp.zeros_like(own_vals))
            probs_t = jnp.exp(dot_nt(own_keys_m, query) + spread(hide_t, local) - lse_row)
            d_v.append(dot_nn(probs_t.astype(BF16), d_attn))
            d_probs_t = dot_nt(own_vals_m, d_attn)
            d_scores_t = (probs_t * (d_probs_t - delta_row)).astype(BF16)
            d_k.append(dot_nn(d_scores_t, query))
        at = pl.ds(pl.multiple_of(c * tokens, tokens), tokens) if not isinstance(c, int) else slice(
            c * tokens, (c + 1) * tokens
        )
        dqkv[at, p * TRIO : p * TRIO + PAIR] = (jnp.where(low, d_q[0], d_q[1]) * SCALE).astype(BF16)
        dqkv[at, p * TRIO + PAIR : p * TRIO + 2 * PAIR] = jnp.where(low, d_k[0], d_k[1]).astype(BF16)
        dqkv[at, p * TRIO + 2 * PAIR : (p + 1) * TRIO] = jnp.where(low, d_v[0], d_v[1]).astype(BF16)

    def y_copy(o, k):
        return remote(
            y_buf.at[o - 1, k], y_got.at[o - 1, k], y_send.at[o - 1, k], y_recv.at[o - 1, k], f_peers[o - 1]
        )

    def product(f, p):
        at = pl.ds(pl.multiple_of(f * rows, rows), rows)
        return dot_nn(nt[at, :], dqkv[:, p * TRIO : (p + 1) * TRIO])

    def pieces(p):
        for j in range(3):
            for r in range(SPLIT):
                yield (p * 3 + j) * SPLIT + r, slice(r * rc, (r + 1) * rc), slice(j * PAIR, (j + 1) * PAIR)

    def send_grads(p):
        for o in range(1, nf):
            part = product((me.f + o) % nf, p).astype(BF16)
            for k, r_at, c_at in pieces(p):
                y_buf[o - 1, k] = part[r_at, c_at]
                y_copy(o, k).start()

    def keep_grads(p):
        part = product(me.f, p)
        for k, r_at, c_at in pieces(p):
            acc[k] = part[r_at, c_at]

    lower = me.z < nz // 2
    depth = jnp.where(lower, me.z, nz - 1 - me.z)
    outer = depth == 0
    has_outer = jnp.logical_not(outer)
    inner = depth == nz // 2 - 1
    not_inner = jnp.logical_not(inner)
    inward = me.at(z=jnp.where(lower, up_z, down_z))
    outward = me.at(z=jnp.where(lower, down_z, up_z))

    def z_copy(k, way):
        return remote(z_buf.at[k], z_got.at[way, k], z_send.at[0, k], z_recv.at[way, k], inward)

    def result_copy(k):
        ref = res.at[me.g, k]
        return remote(ref, ref, z_send.at[1, k], z_recv.at[2, k], outward)

    def g_copy(g, k, way, to):
        return remote(res.at[g, k], res.at[g, k], g_send.at[way, k], g_recv.at[way, k], to)

    def out_copy(g, k):
        p, j, r = k // per_pair, k // SPLIT % 3, k % SPLIT
        at = pl.ds(pl.multiple_of(j * width + g * gw + p * PAIR, PAIR), PAIR)
        return pltpu.make_async_copy(res.at[g, k], grad_out.at[r * rc : (r + 1) * rc, at], o_sem.at[g, k])

    def stage_a(k):
        value = acc[k]
        for o in range(1, nf):
            y_copy(o, k).wait_recv()
            value = value + y_got[o - 1, k].astype(F32)
        acc[k] = value

        @pl.when(outer)
        def _():
            z_buf[k] = acc[k].astype(BF16)
            z_copy(k, 0).start()

    def stage_b(k):
        @pl.when(has_outer)
        def _():
            z_copy(k, 0).wait_recv()
            z_buf[k] = (acc[k] + z_got[0, k].astype(F32)).astype(BF16)

            @pl.when(inner)
            def _():
                z_copy(k, 1).start()

            @pl.when(not_inner)
            def _():
                z_copy(k, 0).start()

    def stage_c(k):
        @pl.when(inner)
        def _():
            z_copy(k, 1).wait_recv()
            res[me.g, k] = (z_buf[k].astype(F32) + z_got[1, k].astype(F32)).astype(BF16)

        @pl.when(not_inner)
        def _():
            result_copy(k).wait_recv()

        @pl.when(has_outer)
        def _():
            result_copy(k).start()

        g_copy(me.g, k, 0, to_x).start()
        g_copy(me.g, k, 1, to_core).start()
        out_copy(me.g, k).start()

    def stage_d(k):
        g_copy(me.g_x, k, 0, to_x).wait_recv()
        g_copy(me.g_x, k, 2, to_core).start()
        out_copy(me.g_x, k).start()

    def stage_e(k):
        g_copy(me.g_core, k, 1, to_core).wait_recv()
        out_copy(me.g_core, k).start()
        g_copy(me.g_far, k, 2, to_core).wait_recv()
        out_copy(me.g_far, k).start()

    def inner_backward(i, carry):
        backward(i, 0)
        return carry

    lax.fori_loop(1, GROUP - 1, inner_backward, 0)
    up_copy.wait_recv()
    down_copy.wait_recv()
    for j in (0, SLOTS - 1):
        unused, parts = d_attn_parts(rbuf[j][8:9, :])
        for p, value in enumerate(parts):
            dattn[j, :, p * PAIR : (p + 1) * PAIR] = value

    def outer_backward(i, carry):
        backward(i * (GROUP - 1), 0)
        return carry

    lax.fori_loop(0, 2, outer_backward, 0)
    send_grads(0)
    keep_grads(0)

    def d_normed(g):
        at = pl.ds(pl.multiple_of(g * tokens, tokens), tokens)
        return dot_nt(dqkv[at, :], wbuf[...])

    def d_copy(at):
        to = to_x if at == 2 else to_core
        return remote(dn_buf.at[at], dn_got.at[at], d_send.at[at], d_recv.at[at], to)

    def far_backward(i, carry):
        backward(jnp.where(i == 0, me.g_far, me.g_x), 1)
        return carry

    def near_backward(i, carry):
        backward(jnp.where(i == 0, me.g_core, me.g), 1)
        return carry

    lax.fori_loop(0, 2, far_backward, 0)
    dn_buf[0] = d_normed(me.g_far).astype(BF16)
    d_copy(0).start()
    dn_acc[...] = d_normed(me.g_x)
    d_copy(0).wait_recv()
    dn_buf[2] = (dn_acc[...] + dn_got[0].astype(F32)).astype(BF16)
    d_copy(2).start()
    stage_a(0)
    lax.fori_loop(0, 2, near_backward, 0)
    send_grads(1)
    stage_a(1)
    dn_buf[1] = d_normed(me.g_core).astype(BF16)
    d_copy(1).start()
    keep_grads(1)
    dn_acc[...] = d_normed(me.g)
    for t in range(2, chunks + LAG_C):
        if t < chunks:
            stage_a(t)
        for k in range(chunks):
            if max(k + LAG_B, 2) == t:
                stage_b(k)
            if max(k + LAG_C, 2) == t:
                stage_c(k)

    d_copy(1).wait_recv()
    d_copy(2).wait_recv()

    def hidden_tile(i, carry):
        at = pl.ds(pl.multiple_of(i * step, step), step)
        d_norm = dn_acc[at, :] + dn_got[1, at, :].astype(F32) + dn_got[2, at, :].astype(F32)
        h_in = hbuf[at, :]
        inv = lax.rsqrt(jnp.mean(h_in * h_in, axis=1, keepdims=True) + EPS)
        d_out = stats[me.g, at, 8:9] * head
        mean = jnp.mean(d_norm * h_in, axis=1, keepdims=True)
        d_hidden_out[at, :] = (d_out + inv * (d_norm - h_in * inv * inv * mean)).astype(BF16)
        return carry

    lax.fori_loop(0, tokens // step, hidden_tile, 0)
    for k in range(chunks):
        stage_d(k)
        if k:
            stage_e(k - 1)
    stage_e(chunks - 1)

    for o in range(1, nf):
        for i in range(4):
            w_copy(i, o).wait_send()
        for i in range(2):
            w_pass_copy(i, o).wait_send()
    for part in range(2):
        for way, to in ((0, to_x), (1, to_core)):
            token_copy(slot, part, way, to).wait_send()
        token_copy(x_slot, part, 2, to_core).wait_send()
    for part in range(2):
        halo_copy(part).wait_send()
        halo_forward(near_halo, part).wait_send()
    for o in range(1, GROUP):
        net_copy(o).wait_send()
    up_copy.wait_send()
    down_copy.wait_send()
    for at in range(3):
        d_copy(at).wait_send()
    for k in range(chunks):
        for o in range(1, nf):
            y_copy(o, k).wait_send()
        z_copy(k, 0).wait_send()
        g_copy(me.g, k, 0, to_x).wait_send()
        g_copy(me.g, k, 1, to_core).wait_send()
        g_copy(me.g_x, k, 2, to_core).wait_send()
        for g in (me.g, me.g_x, me.g_core, me.g_far):
            out_copy(g, k).wait()

    @pl.when(has_outer)
    def _():
        for k in range(chunks):
            result_copy(k).wait_send()


def layer_call(nf, nz, hidden, w, cvec, head, freq, time_idx, cond_mask, noise, blocks, counts):
    tokens, width = hidden.shape
    rows = width // nf
    rc = rows // SPLIT
    chunks = PAIRS * 3 * SPLIT
    gw = width // GROUP
    dma = pltpu.SemaphoreType.DMA
    return pl.pallas_call(
        functools.partial(layer_kernel, nf, nz),
        in_specs=[HBM] * 10,
        out_specs=[VMEM, VMEM],
        out_shape=[
            pltpu.VMEM((rows, 3 * width), BF16),
            pltpu.VMEM((tokens, width), BF16),
        ],
        scratch_shapes=[
            pltpu.VMEM(hidden.shape, BF16),
            pltpu.VMEM(cvec.shape, BF16),
            pltpu.VMEM(head.shape, BF16),
            pltpu.VMEM(freq.shape, F32),
            pltpu.VMEM(time_idx.shape, jnp.int32),
            pltpu.VMEM(cond_mask.shape, jnp.int32),
            pltpu.VMEM(noise.shape, F32),
            pltpu.SMEM(blocks.shape, jnp.int32),
            pltpu.SMEM(counts.shape, jnp.int32),
            pltpu.VMEM((1, width), F32),
            pltpu.VMEM((SLOTS, tokens + 16, width), BF16),
            pltpu.VMEM((width, GROUP * tokens), BF16),
            pltpu.VMEM((width, 3 * gw), BF16),
            pltpu.VMEM((tokens, width), F32),
            pltpu.VMEM((SLOTS, tokens, 3 * gw), BF16),
            pltpu.VMEM((tokens, PAIR), F32),
            pltpu.VMEM((tokens, PAIR), F32),
            pltpu.VMEM((GROUP, 8, 3 * tokens), F32),
            pltpu.VMEM((GROUP, 8, 3 * tokens), F32),
            pltpu.VMEM((GROUP, tokens, gw), BF16),
            pltpu.VMEM((GROUP, tokens, PAIR), F32),
            pltpu.VMEM((GROUP, GROUP, 8, tokens), F32),
            pltpu.VMEM((SLOTS, 16, tokens), F32),
            pltpu.VMEM((SLOTS, tokens, gw), BF16),
            pltpu.VMEM((GROUP * tokens, 3 * gw), BF16),
            pltpu.VMEM((chunks, rc, PAIR), F32),
            pltpu.VMEM((nf - 1, chunks, rc, PAIR), BF16),
            pltpu.VMEM((nf - 1, chunks, rc, PAIR), BF16),
            pltpu.VMEM((chunks, rc, PAIR), BF16),
            pltpu.VMEM((2, chunks, rc, PAIR), BF16),
            pltpu.VMEM((GROUP, chunks, rc, PAIR), BF16),
            pltpu.VMEM((tokens, width), F32),
            pltpu.VMEM((3, tokens, width), BF16),
            pltpu.VMEM((3, tokens, width), BF16),
            dma((nf - 1, 3 * PAIRS)),
            dma((nf - 1, 3 * PAIRS)),
            dma((3 * PAIRS,)),
            dma((3, 2)),
            dma((3, 2)),
            dma((2, 2)),
            dma((2, 2)),
            dma((GROUP - 1,)),
            dma((GROUP - 1,)),
            dma((2,)),
            dma((2,)),
            dma((nf - 1, chunks)),
            dma((nf - 1, chunks)),
            dma((2, chunks)),
            dma((3, chunks)),
            dma((3, chunks)),
            dma((3, chunks)),
            dma((3,)),
            dma((3,)),
            dma((GROUP, chunks)),
            dma((9,)),
        ],
        compiler_params=pltpu.CompilerParams(
            collective_id=0, has_side_effects=True, vmem_limit_bytes=56 << 20
        ),
        name="layer",
    )(hidden, w, cvec, head, freq, time_idx, cond_mask, noise, blocks, counts)


def body(hidden, w_qkv, cond_vec, head_w, blocks, counts, time_idx, cond_mask, noise):
    width = hidden.shape[2]
    half = width // 2
    nf = lax.axis_size("fsdp")
    nz = lax.axis_size("seq") // GROUP
    freq = np.exp(np.float32(-math.log(10000.0)) * np.arange(half, dtype=np.float32) / np.float32(half))
    grad, d_hidden = layer_call(
        nf,
        nz,
        hidden[0],
        w_qkv,
        cond_vec.reshape(width // PAIR, PAIR),
        head_w.reshape(width // PAIR, PAIR),
        jnp.asarray(freq.astype(np.float32))[None, :],
        time_idx,
        cond_mask,
        noise,
        blocks,
        counts,
    )
    return (d_hidden[None], grad.astype(F32))


def solution(mesh):
    return jax.shard_map(
        body,
        mesh=mesh,
        in_specs=(
            P("fsdp", "seq", None),
            P("fsdp", None),
            P(),
            P(),
            P("fsdp", "seq", None),
            P("fsdp", "seq"),
            P("fsdp", "seq"),
            P("fsdp", "seq"),
            P("fsdp", "seq"),
        ),
        out_specs=(P("fsdp", "seq", None), P("fsdp", None)),
        check_vma=False,
    )
```

```python
import functools
import math

import jax
import jax.numpy as jnp
import numpy as np
from jax import lax
from jax.experimental import pallas as pl
from jax.experimental.pallas import tpu as pltpu
from jax.sharding import PartitionSpec as P

HD = 64
BLK = 64
PAIR = 2 * HD
TRIO = 3 * PAIR
GROUP = 4
PAIRS = 2
SLOTS = GROUP + 2
SPLIT = 1
LAG_B = 2
LAG_C = 4
EPS = 1e-05
SCALE = HD ** (-0.5)
NEG = -1e30
F32 = jnp.float32
BF16 = jnp.bfloat16
MESH = pl.DeviceIdType.MESH
ANY = pl.BlockSpec(memory_space=pl.ANY)
HBM = pl.BlockSpec(memory_space=pltpu.HBM)
VMEM = pl.BlockSpec(memory_space=pltpu.VMEM)
SMEM = pl.BlockSpec(memory_space=pltpu.SMEM)


def dot_nt(a, b):
    return lax.dot_general(a, b, (((1,), (1,)), ((), ())), preferred_element_type=F32)


def dot_nn(a, b):
    return jnp.dot(a, b, preferred_element_type=F32)


class Place:
    def __init__(self):
        seq = lax.axis_index("seq")
        self.seq = seq
        self.f = lax.axis_index("fsdp")
        self.z = seq // GROUP
        self.g = seq % GROUP
        self.core = self.g % 2
        self.x = self.g // 2
        self.g_core = self.x * 2 + 1 - self.core
        self.g_x = (1 - self.x) * 2 + self.core
        self.g_far = (1 - self.x) * 2 + 1 - self.core

    def at(self, z=None, g=None, f=None):
        z = self.z if z is None else z
        g = self.g if g is None else g
        f = self.f if f is None else f
        return (z * GROUP + g, f)


def remote(src, dst, send, recv, device):
    return pltpu.make_async_remote_copy(
        src_ref=src, dst_ref=dst, send_sem=send, recv_sem=recv, device_id=device, device_id_type=MESH
    )


def signal(device):
    pl.semaphore_signal(pltpu.get_barrier_semaphore(), inc=1, device_id=device, device_id_type=MESH)


def one_row(ref):
    value = ref[...].astype(F32)
    return jnp.concatenate([value[i : i + 1] for i in range(value.shape[0])], axis=1)


def block_rows(seen, tokens):
    at = lax.broadcasted_iota(jnp.int32, (PAIR, tokens), 0)
    of = lax.broadcasted_iota(jnp.int32, (PAIR, tokens), 1) // BLK
    return dot_nn(seen, jnp.where(at == of, 1.0, 0.0).astype(BF16))


def spread(rows, count):
    return jnp.concatenate(
        [jnp.broadcast_to(rows[b : b + 1], (BLK, rows.shape[1])) for b in range(count)], axis=0
    )


def layer_kernel(
    nf,
    nz,
    hidden_hbm,
    w_ref,
    cvec_hbm,
    head_hbm,
    freq_hbm,
    time_hbm,
    cond_hbm,
    noise_hbm,
    blocks_hbm,
    counts_hbm,
    grad_out,
    d_hidden_out,
    hidden_ref,
    cvec_ref,
    head_ref,
    freq_ref,
    time_ref,
    cond_ref,
    noise_ref,
    blocks_ref,
    counts_ref,
    head_row,
    nbuf,
    nt,
    wbuf,
    hbuf,
    qbuf,
    cols,
    base,
    bias,
    bias_t,
    attn,
    stats,
    mbuf,
    rbuf,
    dattn,
    dqkv,
    acc,
    y_buf,
    y_got,
    z_buf,
    z_got,
    res,
    dn_acc,
    dn_buf,
    dn_got,
    w_send,
    w_recv,
    w_own,
    n_send,
    n_recv,
    h_send,
    h_recv,
    m_send,
    m_recv,
    r_send,
    r_recv,
    y_send,
    y_recv,
    z_send,
    z_recv,
    g_send,
    g_recv,
    d_send,
    d_recv,
    in_sem,
):
    me = Place()
    loads = [
        pltpu.make_async_copy(src, dst, in_sem.at[at])
        for at, (src, dst) in enumerate(
            (
                (hidden_hbm, hidden_ref),
                (cvec_hbm, cvec_ref),
                (head_hbm, head_ref),
                (freq_hbm, freq_ref),
                (time_hbm, time_ref),
                (cond_hbm, cond_ref),
                (noise_hbm, noise_ref),
                (blocks_hbm, blocks_ref),
                (counts_hbm, counts_ref),
            )
        )
    ]
    for copy in loads:
        copy.start()
    tokens, width = hidden_ref.shape
    gw = width // GROUP
    w_rows = w_ref.shape[0]
    total = GROUP * tokens
    window = 3 * tokens
    local = tokens // BLK
    rows = width // nf
    rc = rows // SPLIT
    per_pair = 3 * SPLIT
    chunks = PAIRS * per_pair
    slot = me.g + 1
    lane = lax.broadcasted_iota(jnp.int32, (1, PAIR), 1)
    low = lane < HD

    up_z = (me.z + 1) % nz
    down_z = (me.z + nz - 1) % nz
    f_peers = [me.at(f=(me.f + o) % nf) for o in range(1, nf)]
    g_peers = [me.at(g=(me.g + o) % GROUP) for o in range(1, GROUP)]
    to_x = me.at(g=me.g_x)
    to_core = me.at(g=me.g_core)
    for device in f_peers + g_peers + [me.at(z=up_z), me.at(z=down_z)]:
        signal(device)
    greeted = nf - 1 + GROUP - 1 + 2

    for copy in loads:
        copy.wait()

    pad = jnp.zeros((5, tokens), F32)
    small = jnp.concatenate([time_ref[...].astype(F32), cond_ref[...].astype(F32), noise_ref[...], pad], axis=0)
    cols[...] = jnp.concatenate([small] + [jnp.zeros((PAIR - 8, tokens), F32)], axis=0).T
    step = 32
    cvec = one_row(cvec_ref)
    head_row[...] = one_row(head_ref)
    head = head_row[...]

    def token_tile(i, carry):
        at = pl.ds(pl.multiple_of(i * step, step), step)
        angle = cols[at, 0:1] * freq_ref[...]
        feats = jnp.concatenate([jnp.sin(angle), jnp.cos(angle)], axis=1)
        h_in = hidden_ref[at, :].astype(F32) + cols[at, 1:2] * cvec + feats
        inv = lax.rsqrt(jnp.mean(h_in * h_in, axis=1, keepdims=True) + EPS)
        hbuf[at, :] = h_in
        nbuf[slot, at, :] = (h_in * inv).astype(BF16)
        base[at, :] = jnp.broadcast_to(jnp.sum(h_in * head, axis=1, keepdims=True), (step, PAIR))
        return carry

    half_tiles = tokens // step // 2
    lax.fori_loop(0, half_tiles, token_tile, 0)

    pl.semaphore_wait(pltpu.get_barrier_semaphore(), greeted)

    odd = me.z % 2
    fetched = [odd * 4, odd * 4 + 1, 2, 3]
    passed = [4 - odd * 4, 5 - odd * 4]
    z_mate = me.at(z=me.z + 1 - 2 * odd)

    def w_piece(at):
        col = pl.multiple_of(at % 3 * width + me.g * gw + at // 3 * PAIR, PAIR)
        return w_ref.at[:, pl.ds(col, PAIR)]

    def w_place(f, at):
        f_rows = pl.ds(pl.multiple_of(f * w_rows, w_rows), w_rows)
        return wbuf.at[f_rows, pl.ds(pl.multiple_of(at * PAIR, PAIR), PAIR)]

    def w_copy(i, o):
        at = fetched[i]
        return remote(w_piece(at), w_place(me.f, at), w_send.at[o - 1, i], w_recv.at[o - 1, i], f_peers[o - 1])

    def w_got_copy(i, o):
        ref = w_place((me.f + nf - o) % nf, fetched[i])
        return remote(ref, ref, w_send.at[o - 1, i], w_recv.at[o - 1, i], f_peers[o - 1])

    def w_pass_copy(i, o):
        ref = w_place((me.f + nf - o) % nf, fetched[i])
        return remote(ref, ref, w_send.at[o - 1, 4 + i], w_recv.at[o - 1, 4 + i], z_mate)

    def w_passed_copy(i, o):
        ref = w_place((me.f + nf - o) % nf, passed[i])
        return remote(ref, ref, w_send.at[o - 1, 4 + i], w_recv.at[o - 1, 4 + i], z_mate)

    def w_own_copy(at):
        return pltpu.make_async_copy(w_piece(at), w_place(me.f, at), w_own.at[at])

    for i in range(4):
        for o in range(1, nf):
            w_copy(i, o).start()

    part_rows = tokens // 2

    def token_copy(slot_at, part, way, to):
        at = slice(0, part_rows) if part == 0 else slice(part_rows, tokens + 16)
        return remote(
            nbuf.at[slot_at, at, :], nbuf.at[slot_at, at, :], n_send.at[way, part], n_recv.at[way, part], to
        )

    token_copy(slot, 0, 0, to_x).start()
    token_copy(slot, 0, 1, to_core).start()
    for at in range(3 * PAIRS):
        w_own_copy(at).start()
    lax.fori_loop(half_tiles, 2 * half_tiles, token_tile, 0)

    at_row = lax.broadcasted_iota(jnp.int32, (16, PAIR), 0)
    at_lane = lax.broadcasted_iota(jnp.int32, (16, PAIR), 1)
    seen = jnp.zeros((16, PAIR), F32)
    seen_t = jnp.zeros((16, PAIR), F32)
    all_blocks = nz * GROUP * local
    for b in range(local):
        for j in range(blocks_ref.shape[2]):
            place = blocks_ref[0, b, j] - (me.seq - 1) * local
            place = jnp.where(place < 0, place + all_blocks, place)
            place = jnp.where(place >= all_blocks, place - all_blocks, place)
            place = jnp.where(j <= counts_ref[0, b], place, -1)
            seen = jnp.where(jnp.logical_and(at_row == b, at_lane == place), 1.0, seen)
            seen_t = jnp.where(jnp.logical_and(at_row == place, at_lane == b), 1.0, seen_t)
    nbuf[slot, tokens:, :PAIR] = seen.astype(BF16)
    nbuf[slot, tokens:, PAIR : 2 * PAIR] = seen_t.astype(BF16)
    nbuf[slot, tokens:, 2 * PAIR :] = jnp.zeros((16, width - 2 * PAIR), BF16)

    token_copy(slot, 1, 0, to_x).start()
    token_copy(slot, 1, 1, to_core).start()

    upward = me.core == 1
    halo_slot = jnp.where(upward, GROUP, 1)
    near_halo = jnp.where(upward, 0, SLOTS - 1)
    other_halo = jnp.where(upward, SLOTS - 1, 0)
    halo_to = me.at(z=jnp.where(upward, up_z, down_z))

    def part_of(part):
        return slice(0, part_rows) if part == 0 else slice(part_rows, tokens + 16)

    def halo_copy(part):
        at = part_of(part)
        return remote(
            nbuf.at[halo_slot, at, :], nbuf.at[near_halo, at, :], h_send.at[0, part], h_recv.at[0, part], halo_to
        )

    def halo_forward(slot_at, part):
        ref = nbuf.at[slot_at, part_of(part), :]
        return remote(ref, ref, h_send.at[1, part], h_recv.at[1, part], to_core)

    at_end = me.z == jnp.where(upward, nz - 1, 0)
    early_halo = me.x == me.core

    @pl.when(early_halo)
    def _():
        for part in range(2):
            halo_copy(part).start()

    for i in range(2):
        for o in range(1, nf):
            w_got_copy(i, o).wait_recv()
            w_pass_copy(i, o).start()
    base_row = base[...].T[0:1, :]

    def turn(slot_at):
        at = pl.ds(pl.multiple_of((slot_at - 1) * tokens, tokens), tokens)
        nt[:, at] = nbuf[slot_at, :tokens, :].T

    def project(slot_at):
        qbuf[slot_at] = dot_nn(nbuf[slot_at, :tokens, :], wbuf[...]).astype(BF16)

    core_slot = me.g_core + 1
    x_slot = me.g_x + 1
    far_slot = me.g_far + 1
    turn(slot)
    for part in range(2):
        token_copy(core_slot, part, 1, to_core).wait_recv()
    turn(core_slot)
    token_copy(x_slot, 0, 0, to_x).wait_recv()
    token_copy(x_slot, 0, 2, to_core).start()

    for i in range(2):
        for o in range(1, nf):
            w_passed_copy(i, o).wait_recv()
            w_got_copy(2 + i, o).wait_recv()
    for at in range(3 * PAIRS):
        w_own_copy(at).wait()
    project(slot)
    project(core_slot)
    token_copy(x_slot, 1, 0, to_x).wait_recv()
    token_copy(x_slot, 1, 2, to_core).start()

    @pl.when(jnp.logical_not(early_halo))
    def _():
        for part in range(2):
            halo_copy(part).start()

    project(x_slot)
    turn(x_slot)
    for part in range(2):
        token_copy(far_slot, part, 2, to_core).wait_recv()
    project(far_slot)
    turn(far_slot)

    def fill_bias(c):
        visible = block_rows(nbuf[c + 1, tokens:, :PAIR], window)
        bias[c] = jnp.where(visible[:8] > 0.5, 0.0, NEG)

    def fill_bias_t(c):
        parts = []
        for s in range(3):
            from_slot = block_rows(nbuf[c + s, tokens:, PAIR : 2 * PAIR], tokens)
            parts.append(from_slot[(2 - s) * local : (3 - s) * local])
        visible = jnp.concatenate(parts, axis=1)
        bias_t[c, :local, :] = jnp.where(visible > 0.5, 0.0, NEG)

    head_group = head_row[0:1, pl.ds(pl.multiple_of(me.g * gw, gw), gw)]
    head_rows = jnp.broadcast_to(head_group, (16, gw)).astype(BF16)

    def forward(c):
        fill_bias(c)
        hide = bias[c]
        net = jnp.zeros((16, tokens), F32)
        found = jnp.zeros((tokens, PAIR), F32)
        for p in range(PAIRS):
            q_part = slice(p * TRIO, p * TRIO + PAIR)
            k_part = slice(p * TRIO + PAIR, p * TRIO + 2 * PAIR)
            v_part = slice(p * TRIO + 2 * PAIR, (p + 1) * TRIO)
            query = qbuf[c + 1, :, q_part] * jnp.asarray(SCALE, BF16)
            keys = qbuf[pl.ds(c, 3), :, k_part].reshape(window, PAIR)
            vals = qbuf[pl.ds(c, 3), :, v_part].reshape(window, PAIR)
            outs = []
            for half in range(2):
                mine = low if half == 0 else jnp.logical_not(low)
                scores = dot_nt(jnp.where(mine, query, jnp.zeros_like(query)), keys) + spread(hide, local)
                top = jnp.max(scores, axis=1, keepdims=True)
                expo = jnp.exp(scores - top)
                norm = jnp.sum(expo, axis=1, keepdims=True)
                probs_b = (expo * (1.0 / norm)).astype(BF16)
                outs.append(dot_nn(probs_b, vals))
                found = jnp.where(lane == 2 * p + half, top + jnp.log(norm), found)
            value = jnp.where(low, outs[0], outs[1]).astype(BF16)
            attn[c, :, p * PAIR : (p + 1) * PAIR] = value
            net = net + dot_nt(head_rows[:, p * PAIR : (p + 1) * PAIR], value)
        stats[c] = found
        mbuf[0, c] = net[:8]

    def inner_chunk(i, carry):
        forward(i)
        return carry

    lax.fori_loop(1, GROUP - 1, inner_chunk, 0)
    for part in range(2):
        halo_copy(part).wait_recv()
        halo_forward(near_halo, part).start()
    project(near_halo)
    for part in range(2):
        halo_forward(other_halo, part).wait_recv()
    project(other_halo)

    def outer_chunk(i, carry):
        forward(i * (GROUP - 1))
        return carry

    lax.fori_loop(0, 2, outer_chunk, 0)

    in_row = lax.broadcasted_iota(jnp.int32, (8, tokens), 0)
    for c in range(GROUP):
        mbuf[0, c] = jnp.where(in_row == 0, mbuf[0, c], 0.0)
    extra = jnp.where(
        in_row == 0, base_row + noise_ref[...], jnp.where(in_row == 1, 2.0 * (1.0 - small[1:2, :]), 0.0)
    )
    mbuf[0, me.g] = mbuf[0, me.g] + extra

    def net_copy(o):
        return remote(mbuf.at[0], mbuf.at[o], m_send.at[o - 1], m_recv.at[o - 1], g_peers[o - 1])

    for o in range(1, GROUP):
        net_copy(o).start()
    for c in range(GROUP):
        fill_bias_t(c)
    for o in range(1, GROUP):
        net_copy(o).wait_recv()

    def d_attn_parts(row):
        col = jnp.broadcast_to(row, (PAIR, tokens)).T
        return col, [(col * head_group[:, p * PAIR : (p + 1) * PAIR]).astype(BF16) for p in range(PAIRS)]

    def finish_stats(c):
        msg = mbuf[0, c] + mbuf[1, c] + mbuf[2, c] + mbuf[3, c]
        col, parts = d_attn_parts(msg[0:1] * msg[1:2])
        full = jnp.where(lane == 8, col, stats[c])
        for p, value in enumerate(parts):
            dattn[c + 1, :, p * PAIR : (p + 1) * PAIR] = value
            prod = value.astype(F32) * attn[c, :, p * PAIR : (p + 1) * PAIR].astype(F32)
            sum_low = jnp.sum(jnp.where(low, prod, 0.0), axis=1, keepdims=True)
            sum_high = jnp.sum(jnp.where(low, 0.0, prod), axis=1, keepdims=True)
            full = jnp.where(lane == 4 + 2 * p, sum_low, full)
            full = jnp.where(lane == 5 + 2 * p, sum_high, full)
        stats[c] = full
        rbuf[c + 1] = full.T[:16, :]

    up_copy = remote(rbuf.at[GROUP], rbuf.at[0], r_send.at[0], r_recv.at[0], me.at(z=up_z))
    down_copy = remote(rbuf.at[1], rbuf.at[SLOTS - 1], r_send.at[1], r_recv.at[1], me.at(z=down_z))
    finish_stats(0)
    down_copy.start()
    finish_stats(GROUP - 1)
    up_copy.start()
    for c in range(1, GROUP - 1):
        finish_stats(c)

    def backward(c, p):
        q_part = slice(p * TRIO, p * TRIO + PAIR)
        k_part = slice(p * TRIO + PAIR, p * TRIO + 2 * PAIR)
        v_part = slice(p * TRIO + 2 * PAIR, (p + 1) * TRIO)
        a_part = slice(p * PAIR, (p + 1) * PAIR)
        hide = bias[c]
        hide_t = bias_t[c]
        found = stats[c]
        scale = jnp.asarray(SCALE, BF16)
        query = qbuf[pl.ds(c, 3), :, q_part].reshape(window, PAIR) * scale
        own_query = qbuf[c + 1, :, q_part] * scale
        keys = qbuf[pl.ds(c, 3), :, k_part].reshape(window, PAIR)
        vals = qbuf[pl.ds(c, 3), :, v_part].reshape(window, PAIR)
        own_keys = qbuf[c + 1, :, k_part]
        own_vals = qbuf[c + 1, :, v_part]
        d_attn = dattn[pl.ds(c, 3), :, a_part].reshape(window, PAIR)
        own_d_attn = dattn[c + 1, :, a_part]
        rows_of = [rbuf[c + s] for s in range(3)]
        d_q, d_k, d_v = [], [], []
        for half in range(2):
            mine = low if half == 0 else jnp.logical_not(low)
            h = 2 * p + half
            lse = found[:, h : h + 1]
            delta = found[:, 4 + h : 5 + h]
            probs = jnp.exp(
                dot_nt(jnp.where(mine, own_query, jnp.zeros_like(own_query)), keys) + spread(hide, local) - lse
            )
            d_probs = dot_nt(jnp.where(mine, own_d_attn, jnp.zeros_like(own_d_attn)), vals)
            d_scores = (probs * (d_probs - delta)).astype(BF16)
            d_q.append(dot_nn(d_scores, keys))
            lse_row = jnp.concatenate([r[h : h + 1] for r in rows_of], axis=1)
            delta_row = jnp.concatenate([r[4 + h : 5 + h] for r in rows_of], axis=1)
            own_keys_m = jnp.where(mine, own_keys, jnp.zeros_like(own_keys))
            own_vals_m = jnp.where(mine, own_vals, jnp.zeros_like(own_vals))
            probs_t = jnp.exp(dot_nt(own_keys_m, query) + spread(hide_t, local) - lse_row)
            d_v.append(dot_nn(probs_t.astype(BF16), d_attn))
            d_probs_t = dot_nt(own_vals_m, d_attn)
            d_scores_t = (probs_t * (d_probs_t - delta_row)).astype(BF16)
            d_k.append(dot_nn(d_scores_t, query))
        at = pl.ds(pl.multiple_of(c * tokens, tokens), tokens) if not isinstance(c, int) else slice(
            c * tokens, (c + 1) * tokens
        )
        dqkv[at, p * TRIO : p * TRIO + PAIR] = (jnp.where(low, d_q[0], d_q[1]) * SCALE).astype(BF16)
        dqkv[at, p * TRIO + PAIR : p * TRIO + 2 * PAIR] = jnp.where(low, d_k[0], d_k[1]).astype(BF16)
        dqkv[at, p * TRIO + 2 * PAIR : (p + 1) * TRIO] = jnp.where(low, d_v[0], d_v[1]).astype(BF16)

    def y_copy(o, k):
        return remote(
            y_buf.at[o - 1, k], y_got.at[o - 1, k], y_send.at[o - 1, k], y_recv.at[o - 1, k], f_peers[o - 1]
        )

    def product(f, p):
        at = pl.ds(pl.multiple_of(f * rows, rows), rows)
        return dot_nn(nt[at, :], dqkv[:, p * TRIO : (p + 1) * TRIO])

    def pieces(p):
        for j in range(3):
            for r in range(SPLIT):
                yield (p * 3 + j) * SPLIT + r, slice(r * rc, (r + 1) * rc), slice(j * PAIR, (j + 1) * PAIR)

    def send_grads(p):
        for o in range(1, nf):
            part = product((me.f + o) % nf, p).astype(BF16)
            for k, r_at, c_at in pieces(p):
                y_buf[o - 1, k] = part[r_at, c_at]
                y_copy(o, k).start()

    def keep_grads(p):
        part = product(me.f, p)
        for k, r_at, c_at in pieces(p):
            acc[k] = part[r_at, c_at]

    lower = me.z < nz // 2
    depth = jnp.where(lower, me.z, nz - 1 - me.z)
    outer = depth == 0
    has_outer = jnp.logical_not(outer)
    inner = depth == nz // 2 - 1
    not_inner = jnp.logical_not(inner)
    inward = me.at(z=jnp.where(lower, up_z, down_z))
    outward = me.at(z=jnp.where(lower, down_z, up_z))

    def z_copy(k, way):
        return remote(z_buf.at[k], z_got.at[way, k], z_send.at[0, k], z_recv.at[way, k], inward)

    def result_copy(k):
        ref = res.at[me.g, k]
        return remote(ref, ref, z_send.at[1, k], z_recv.at[2, k], outward)

    def g_copy(g, k, way, to):
        return remote(res.at[g, k], res.at[g, k], g_send.at[way, k], g_recv.at[way, k], to)

    def place_result(g, k):
        p, j, r = k // per_pair, k // SPLIT % 3, k % SPLIT
        at = pl.ds(pl.multiple_of(j * width + g * gw + p * PAIR, PAIR), PAIR)
        grad_out[r * rc : (r + 1) * rc, at] = res[g, k].astype(F32)

    def stage_a(k):
        value = acc[k]
        for o in range(1, nf):
            y_copy(o, k).wait_recv()
            value = value + y_got[o - 1, k].astype(F32)
        acc[k] = value

        @pl.when(outer)
        def _():
            z_buf[k] = acc[k].astype(BF16)
            z_copy(k, 0).start()

    def stage_b(k):
        @pl.when(has_outer)
        def _():
            z_copy(k, 0).wait_recv()
            z_buf[k] = (acc[k] + z_got[0, k].astype(F32)).astype(BF16)

            @pl.when(inner)
            def _():
                z_copy(k, 1).start()

            @pl.when(not_inner)
            def _():
                z_copy(k, 0).start()

    def stage_c(k):
        @pl.when(inner)
        def _():
            z_copy(k, 1).wait_recv()
            res[me.g, k] = (z_buf[k].astype(F32) + z_got[1, k].astype(F32)).astype(BF16)

        @pl.when(not_inner)
        def _():
            result_copy(k).wait_recv()

        @pl.when(has_outer)
        def _():
            result_copy(k).start()

        g_copy(me.g, k, 0, to_x).start()
        g_copy(me.g, k, 1, to_core).start()
        place_result(me.g, k)

    def stage_d(k):
        g_copy(me.g_x, k, 0, to_x).wait_recv()
        g_copy(me.g_x, k, 2, to_core).start()
        place_result(me.g_x, k)

    def stage_e(k):
        g_copy(me.g_core, k, 1, to_core).wait_recv()
        place_result(me.g_core, k)
        g_copy(me.g_far, k, 2, to_core).wait_recv()
        place_result(me.g_far, k)

    def inner_backward(i, carry):
        backward(i, 0)
        return carry

    lax.fori_loop(1, GROUP - 1, inner_backward, 0)
    up_copy.wait_recv()
    down_copy.wait_recv()
    for j in (0, SLOTS - 1):
        unused, parts = d_attn_parts(rbuf[j][8:9, :])
        for p, value in enumerate(parts):
            dattn[j, :, p * PAIR : (p + 1) * PAIR] = value

    def outer_backward(i, carry):
        backward(i * (GROUP - 1), 0)
        return carry

    lax.fori_loop(0, 2, outer_backward, 0)
    send_grads(0)
    keep_grads(0)

    def d_normed(g):
        at = pl.ds(pl.multiple_of(g * tokens, tokens), tokens)
        return dot_nt(dqkv[at, :], wbuf[...])

    def d_copy(at):
        to = to_x if at == 2 else to_core
        return remote(dn_buf.at[at], dn_got.at[at], d_send.at[at], d_recv.at[at], to)

    def far_backward(i, carry):
        backward(jnp.where(i == 0, me.g_far, me.g_x), 1)
        return carry

    def near_backward(i, carry):
        backward(jnp.where(i == 0, me.g_core, me.g), 1)
        return carry

    lax.fori_loop(0, 2, far_backward, 0)
    dn_buf[0] = d_normed(me.g_far).astype(BF16)
    d_copy(0).start()
    dn_acc[...] = d_normed(me.g_x)
    d_copy(0).wait_recv()
    dn_buf[2] = (dn_acc[...] + dn_got[0].astype(F32)).astype(BF16)
    d_copy(2).start()
    stage_a(0)
    lax.fori_loop(0, 2, near_backward, 0)
    send_grads(1)
    stage_a(1)
    dn_buf[1] = d_normed(me.g_core).astype(BF16)
    d_copy(1).start()
    keep_grads(1)
    dn_acc[...] = d_normed(me.g)
    for t in range(2, chunks + LAG_C):
        if t < chunks:
            stage_a(t)
        for k in range(chunks):
            if max(k + LAG_B, 2) == t:
                stage_b(k)
            if max(k + LAG_C, 2) == t:
                stage_c(k)

    d_copy(1).wait_recv()
    d_copy(2).wait_recv()

    def hidden_tile(i, carry):
        at = pl.ds(pl.multiple_of(i * step, step), step)
        d_norm = dn_acc[at, :] + dn_got[1, at, :].astype(F32) + dn_got[2, at, :].astype(F32)
        h_in = hbuf[at, :]
        inv = lax.rsqrt(jnp.mean(h_in * h_in, axis=1, keepdims=True) + EPS)
        d_out = stats[me.g, at, 8:9] * head
        mean = jnp.mean(d_norm * h_in, axis=1, keepdims=True)
        d_hidden_out[at, :] = (d_out + inv * (d_norm - h_in * inv * inv * mean)).astype(BF16)
        return carry

    lax.fori_loop(0, tokens // step, hidden_tile, 0)
    for k in range(chunks):
        stage_d(k)
        if k:
            stage_e(k - 1)
    stage_e(chunks - 1)

    for o in range(1, nf):
        for i in range(4):
            w_copy(i, o).wait_send()
        for i in range(2):
            w_pass_copy(i, o).wait_send()
    for part in range(2):
        for way, to in ((0, to_x), (1, to_core)):
            token_copy(slot, part, way, to).wait_send()
        token_copy(x_slot, part, 2, to_core).wait_send()
    for part in range(2):
        halo_copy(part).wait_send()
        halo_forward(near_halo, part).wait_send()
    for o in range(1, GROUP):
        net_copy(o).wait_send()
    up_copy.wait_send()
    down_copy.wait_send()
    for at in range(3):
        d_copy(at).wait_send()
    for k in range(chunks):
        for o in range(1, nf):
            y_copy(o, k).wait_send()
        z_copy(k, 0).wait_send()
        g_copy(me.g, k, 0, to_x).wait_send()
        g_copy(me.g, k, 1, to_core).wait_send()
        g_copy(me.g_x, k, 2, to_core).wait_send()

    @pl.when(has_outer)
    def _():
        for k in range(chunks):
            result_copy(k).wait_send()


def layer_call(nf, nz, hidden, w, cvec, head, freq, time_idx, cond_mask, noise, blocks, counts):
    tokens, width = hidden.shape
    rows = width // nf
    rc = rows // SPLIT
    chunks = PAIRS * 3 * SPLIT
    gw = width // GROUP
    dma = pltpu.SemaphoreType.DMA
    return pl.pallas_call(
        functools.partial(layer_kernel, nf, nz),
        in_specs=[HBM] * 10,
        out_specs=[VMEM, VMEM],
        out_shape=[
            pltpu.VMEM((rows, 3 * width), F32),
            pltpu.VMEM((tokens, width), BF16),
        ],
        scratch_shapes=[
            pltpu.VMEM(hidden.shape, BF16),
            pltpu.VMEM(cvec.shape, BF16),
            pltpu.VMEM(head.shape, BF16),
            pltpu.VMEM(freq.shape, F32),
            pltpu.VMEM(time_idx.shape, jnp.int32),
            pltpu.VMEM(cond_mask.shape, jnp.int32),
            pltpu.VMEM(noise.shape, F32),
            pltpu.SMEM(blocks.shape, jnp.int32),
            pltpu.SMEM(counts.shape, jnp.int32),
            pltpu.VMEM((1, width), F32),
            pltpu.VMEM((SLOTS, tokens + 16, width), BF16),
            pltpu.VMEM((width, GROUP * tokens), BF16),
            pltpu.VMEM((width, 3 * gw), BF16),
            pltpu.VMEM((tokens, width), F32),
            pltpu.VMEM((SLOTS, tokens, 3 * gw), BF16),
            pltpu.VMEM((tokens, PAIR), F32),
            pltpu.VMEM((tokens, PAIR), F32),
            pltpu.VMEM((GROUP, 8, 3 * tokens), F32),
            pltpu.VMEM((GROUP, 8, 3 * tokens), F32),
            pltpu.VMEM((GROUP, tokens, gw), BF16),
            pltpu.VMEM((GROUP, tokens, PAIR), F32),
            pltpu.VMEM((GROUP, GROUP, 8, tokens), F32),
            pltpu.VMEM((SLOTS, 16, tokens), F32),
            pltpu.VMEM((SLOTS, tokens, gw), BF16),
            pltpu.VMEM((GROUP * tokens, 3 * gw), BF16),
            pltpu.VMEM((chunks, rc, PAIR), F32),
            pltpu.VMEM((nf - 1, chunks, rc, PAIR), BF16),
            pltpu.VMEM((nf - 1, chunks, rc, PAIR), BF16),
            pltpu.VMEM((chunks, rc, PAIR), BF16),
            pltpu.VMEM((2, chunks, rc, PAIR), BF16),
            pltpu.VMEM((GROUP, chunks, rc, PAIR), BF16),
            pltpu.VMEM((tokens, width), F32),
            pltpu.VMEM((3, tokens, width), BF16),
            pltpu.VMEM((3, tokens, width), BF16),
            dma((nf - 1, 3 * PAIRS)),
            dma((nf - 1, 3 * PAIRS)),
            dma((3 * PAIRS,)),
            dma((3, 2)),
            dma((3, 2)),
            dma((2, 2)),
            dma((2, 2)),
            dma((GROUP - 1,)),
            dma((GROUP - 1,)),
            dma((2,)),
            dma((2,)),
            dma((nf - 1, chunks)),
            dma((nf - 1, chunks)),
            dma((2, chunks)),
            dma((3, chunks)),
            dma((3, chunks)),
            dma((3, chunks)),
            dma((3,)),
            dma((3,)),
            dma((9,)),
        ],
        compiler_params=pltpu.CompilerParams(
            collective_id=0, has_side_effects=True, vmem_limit_bytes=54 << 20
        ),
        name="layer",
    )(hidden, w, cvec, head, freq, time_idx, cond_mask, noise, blocks, counts)


def body(hidden, w_qkv, cond_vec, head_w, blocks, counts, time_idx, cond_mask, noise):
    width = hidden.shape[2]
    half = width // 2
    nf = lax.axis_size("fsdp")
    nz = lax.axis_size("seq") // GROUP
    freq = np.exp(np.float32(-math.log(10000.0)) * np.arange(half, dtype=np.float32) / np.float32(half))
    grad, d_hidden = layer_call(
        nf,
        nz,
        hidden[0],
        w_qkv,
        cond_vec.reshape(width // PAIR, PAIR),
        head_w.reshape(width // PAIR, PAIR),
        jnp.asarray(freq.astype(np.float32))[None, :],
        time_idx,
        cond_mask,
        noise,
        blocks,
        counts,
    )
    return (d_hidden[None], grad)


def solution(mesh):
    return jax.shard_map(
        body,
        mesh=mesh,
        in_specs=(
            P("fsdp", "seq", None),
            P("fsdp", None),
            P(),
            P(),
            P("fsdp", "seq", None),
            P("fsdp", "seq"),
            P("fsdp", "seq"),
            P("fsdp", "seq"),
            P("fsdp", "seq"),
        ),
        out_specs=(P("fsdp", "seq", None), P("fsdp", None)),
        check_vma=False,
    )
```

```python
import functools
import math

import jax
import jax.numpy as jnp
import numpy as np
from jax import lax
from jax.experimental import pallas as pl
from jax.experimental.pallas import tpu as pltpu
from jax.sharding import PartitionSpec as P

HD = 64
BLK = 64
PAIR = 2 * HD
TRIO = 3 * PAIR
GROUP = 4
PAIRS = 2
SLOTS = GROUP + 2
SPLIT = 1
LAG_B = 2
LAG_C = 4
EPS = 1e-05
SCALE = HD ** (-0.5)
NEG = -1e30
F32 = jnp.float32
BF16 = jnp.bfloat16
MESH = pl.DeviceIdType.MESH
ANY = pl.BlockSpec(memory_space=pl.ANY)
HBM = pl.BlockSpec(memory_space=pltpu.HBM)
VMEM = pl.BlockSpec(memory_space=pltpu.VMEM)
SMEM = pl.BlockSpec(memory_space=pltpu.SMEM)


def dot_nt(a, b):
    return lax.dot_general(a, b, (((1,), (1,)), ((), ())), preferred_element_type=F32)


def dot_nn(a, b):
    return jnp.dot(a, b, preferred_element_type=F32)


class Place:
    def __init__(self):
        seq = lax.axis_index("seq")
        self.seq = seq
        self.f = lax.axis_index("fsdp")
        self.z = seq // GROUP
        self.g = seq % GROUP
        self.core = self.g % 2
        self.x = self.g // 2
        self.g_core = self.x * 2 + 1 - self.core
        self.g_x = (1 - self.x) * 2 + self.core
        self.g_far = (1 - self.x) * 2 + 1 - self.core

    def at(self, z=None, g=None, f=None):
        z = self.z if z is None else z
        g = self.g if g is None else g
        f = self.f if f is None else f
        return (z * GROUP + g, f)


def remote(src, dst, send, recv, device):
    return pltpu.make_async_remote_copy(
        src_ref=src, dst_ref=dst, send_sem=send, recv_sem=recv, device_id=device, device_id_type=MESH
    )


def signal(device):
    pl.semaphore_signal(pltpu.get_barrier_semaphore(), inc=1, device_id=device, device_id_type=MESH)


def one_row(ref):
    value = ref[...].astype(F32)
    return jnp.concatenate([value[i : i + 1] for i in range(value.shape[0])], axis=1)


def block_rows(seen, tokens):
    at = lax.broadcasted_iota(jnp.int32, (PAIR, tokens), 0)
    of = lax.broadcasted_iota(jnp.int32, (PAIR, tokens), 1) // BLK
    return dot_nn(seen, jnp.where(at == of, 1.0, 0.0).astype(BF16))


def spread(rows, count):
    return jnp.concatenate(
        [jnp.broadcast_to(rows[b : b + 1], (BLK, rows.shape[1])) for b in range(count)], axis=0
    )


def layer_kernel(
    nf,
    nz,
    hidden_hbm,
    w_ref,
    cvec_hbm,
    head_hbm,
    freq_hbm,
    time_hbm,
    cond_hbm,
    noise_hbm,
    blocks_hbm,
    counts_hbm,
    grad_out,
    d_hidden_out,
    hidden_ref,
    cvec_ref,
    head_ref,
    freq_ref,
    time_ref,
    cond_ref,
    noise_ref,
    blocks_ref,
    counts_ref,
    head_row,
    nbuf,
    nt,
    wbuf,
    hbuf,
    qbuf,
    cols,
    base,
    bias,
    bias_t,
    attn,
    stats,
    mbuf,
    rbuf,
    dattn,
    dqkv,
    acc,
    y_buf,
    y_got,
    z_buf,
    z_got,
    res,
    dn_acc,
    dn_buf,
    dn_got,
    w_send,
    w_recv,
    w_own,
    n_send,
    n_recv,
    h_send,
    h_recv,
    m_send,
    m_recv,
    r_send,
    r_recv,
    y_send,
    y_recv,
    z_send,
    z_recv,
    g_send,
    g_recv,
    d_send,
    d_recv,
    in_sem,
):
    me = Place()
    loads = [
        pltpu.make_async_copy(src, dst, in_sem.at[at])
        for at, (src, dst) in enumerate(
            (
                (hidden_hbm, hidden_ref),
                (cvec_hbm, cvec_ref),
                (head_hbm, head_ref),
                (freq_hbm, freq_ref),
                (time_hbm, time_ref),
                (cond_hbm, cond_ref),
                (noise_hbm, noise_ref),
                (blocks_hbm, blocks_ref),
                (counts_hbm, counts_ref),
            )
        )
    ]
    for copy in loads:
        copy.start()
    tokens, width = hidden_ref.shape
    gw = width // GROUP
    w_rows = w_ref.shape[0]
    total = GROUP * tokens
    window = 3 * tokens
    local = tokens // BLK
    rows = width // nf
    rc = rows // SPLIT
    per_pair = 3 * SPLIT
    chunks = PAIRS * per_pair
    slot = me.g + 1
    lane = lax.broadcasted_iota(jnp.int32, (1, PAIR), 1)
    low = lane < HD

    up_z = (me.z + 1) % nz
    down_z = (me.z + nz - 1) % nz
    f_peers = [me.at(f=(me.f + o) % nf) for o in range(1, nf)]
    g_peers = [me.at(g=(me.g + o) % GROUP) for o in range(1, GROUP)]
    to_x = me.at(g=me.g_x)
    to_core = me.at(g=me.g_core)
    for device in f_peers + g_peers + [me.at(z=up_z), me.at(z=down_z)]:
        signal(device)
    greeted = nf - 1 + GROUP - 1 + 2

    for copy in loads:
        copy.wait()

    pad = jnp.zeros((5, tokens), F32)
    small = jnp.concatenate([time_ref[...].astype(F32), cond_ref[...].astype(F32), noise_ref[...], pad], axis=0)
    cols[...] = jnp.concatenate([small] + [jnp.zeros((PAIR - 8, tokens), F32)], axis=0).T
    step = 32
    cvec = one_row(cvec_ref)
    head_row[...] = one_row(head_ref)
    head = head_row[...]

    def token_tile(i, carry):
        at = pl.ds(pl.multiple_of(i * step, step), step)
        angle = cols[at, 0:1] * freq_ref[...]
        feats = jnp.concatenate([jnp.sin(angle), jnp.cos(angle)], axis=1)
        h_in = hidden_ref[at, :].astype(F32) + cols[at, 1:2] * cvec + feats
        inv = lax.rsqrt(jnp.mean(h_in * h_in, axis=1, keepdims=True) + EPS)
        hbuf[at, :] = h_in
        nbuf[slot, at, :] = (h_in * inv).astype(BF16)
        base[at, :] = jnp.broadcast_to(jnp.sum(h_in * head, axis=1, keepdims=True), (step, PAIR))
        return carry

    half_tiles = tokens // step // 2
    lax.fori_loop(0, half_tiles, token_tile, 0)

    pl.semaphore_wait(pltpu.get_barrier_semaphore(), greeted)

    odd = me.z % 2
    fetched = [odd * 4, odd * 4 + 1, 2, 3]
    passed = [4 - odd * 4, 5 - odd * 4]
    z_mate = me.at(z=me.z + 1 - 2 * odd)

    def w_piece(at):
        col = pl.multiple_of(at % 3 * width + me.g * gw + at // 3 * PAIR, PAIR)
        return w_ref.at[:, pl.ds(col, PAIR)]

    def w_place(f, at):
        f_rows = pl.ds(pl.multiple_of(f * w_rows, w_rows), w_rows)
        return wbuf.at[f_rows, pl.ds(pl.multiple_of(at * PAIR, PAIR), PAIR)]

    def w_copy(i, o):
        at = fetched[i]
        return remote(w_piece(at), w_place(me.f, at), w_send.at[o - 1, i], w_recv.at[o - 1, i], f_peers[o - 1])

    def w_got_copy(i, o):
        ref = w_place((me.f + nf - o) % nf, fetched[i])
        return remote(ref, ref, w_send.at[o - 1, i], w_recv.at[o - 1, i], f_peers[o - 1])

    def w_pass_copy(i, o):
        ref = w_place((me.f + nf - o) % nf, fetched[i])
        return remote(ref, ref, w_send.at[o - 1, 4 + i], w_recv.at[o - 1, 4 + i], z_mate)

    def w_passed_copy(i, o):
        ref = w_place((me.f + nf - o) % nf, passed[i])
        return remote(ref, ref, w_send.at[o - 1, 4 + i], w_recv.at[o - 1, 4 + i], z_mate)

    def w_own_copy(at):
        return pltpu.make_async_copy(w_piece(at), w_place(me.f, at), w_own.at[at])

    for i in range(4):
        for o in range(1, nf):
            w_copy(i, o).start()

    part_rows = tokens // 2

    def token_copy(slot_at, part, way, to):
        at = slice(0, part_rows) if part == 0 else slice(part_rows, tokens + 16)
        return remote(
            nbuf.at[slot_at, at, :], nbuf.at[slot_at, at, :], n_send.at[way, part], n_recv.at[way, part], to
        )

    token_copy(slot, 0, 0, to_x).start()
    token_copy(slot, 0, 1, to_core).start()
    for at in range(3 * PAIRS):
        w_own_copy(at).start()
    lax.fori_loop(half_tiles, 2 * half_tiles, token_tile, 0)

    at_row = lax.broadcasted_iota(jnp.int32, (16, PAIR), 0)
    at_lane = lax.broadcasted_iota(jnp.int32, (16, PAIR), 1)
    seen = jnp.zeros((16, PAIR), F32)
    seen_t = jnp.zeros((16, PAIR), F32)
    all_blocks = nz * GROUP * local
    for b in range(local):
        for j in range(blocks_ref.shape[2]):
            place = blocks_ref[0, b, j] - (me.seq - 1) * local
            place = jnp.where(place < 0, place + all_blocks, place)
            place = jnp.where(place >= all_blocks, place - all_blocks, place)
            place = jnp.where(j <= counts_ref[0, b], place, -1)
            seen = jnp.where(jnp.logical_and(at_row == b, at_lane == place), 1.0, seen)
            seen_t = jnp.where(jnp.logical_and(at_row == place, at_lane == b), 1.0, seen_t)
    nbuf[slot, tokens:, :PAIR] = seen.astype(BF16)
    nbuf[slot, tokens:, PAIR : 2 * PAIR] = seen_t.astype(BF16)
    nbuf[slot, tokens:, 2 * PAIR :] = jnp.zeros((16, width - 2 * PAIR), BF16)

    token_copy(slot, 1, 0, to_x).start()
    token_copy(slot, 1, 1, to_core).start()

    upward = me.core == 1
    halo_slot = jnp.where(upward, GROUP, 1)
    near_halo = jnp.where(upward, 0, SLOTS - 1)
    other_halo = jnp.where(upward, SLOTS - 1, 0)
    halo_to = me.at(z=jnp.where(upward, up_z, down_z))

    def halo_copy():
        return remote(nbuf.at[halo_slot], nbuf.at[near_halo], h_send.at[0], h_recv.at[0], halo_to)

    def halo_forward(slot_at):
        return remote(nbuf.at[slot_at], nbuf.at[slot_at], h_send.at[1], h_recv.at[1], to_core)

    at_end = me.z == jnp.where(upward, nz - 1, 0)
    early_halo = me.x == me.core

    @pl.when(early_halo)
    def _():
        halo_copy().start()

    for i in range(2):
        for o in range(1, nf):
            w_got_copy(i, o).wait_recv()
            w_pass_copy(i, o).start()
    base_row = base[...].T[0:1, :]

    def turn(slot_at):
        at = pl.ds(pl.multiple_of((slot_at - 1) * tokens, tokens), tokens)
        nt[:, at] = nbuf[slot_at, :tokens, :].T

    def project(slot_at):
        qbuf[slot_at] = dot_nn(nbuf[slot_at, :tokens, :], wbuf[...]).astype(BF16)

    core_slot = me.g_core + 1
    x_slot = me.g_x + 1
    far_slot = me.g_far + 1
    turn(slot)
    for part in range(2):
        token_copy(core_slot, part, 1, to_core).wait_recv()
    turn(core_slot)
    token_copy(x_slot, 0, 0, to_x).wait_recv()
    token_copy(x_slot, 0, 2, to_core).start()

    for i in range(2):
        for o in range(1, nf):
            w_passed_copy(i, o).wait_recv()
            w_got_copy(2 + i, o).wait_recv()
    for at in range(3 * PAIRS):
        w_own_copy(at).wait()
    project(slot)
    project(core_slot)
    token_copy(x_slot, 1, 0, to_x).wait_recv()
    token_copy(x_slot, 1, 2, to_core).start()

    @pl.when(jnp.logical_not(early_halo))
    def _():
        halo_copy().start()

    project(x_slot)
    turn(x_slot)
    for part in range(2):
        token_copy(far_slot, part, 2, to_core).wait_recv()
    project(far_slot)
    turn(far_slot)

    def fill_bias(c):
        visible = block_rows(nbuf[c + 1, tokens:, :PAIR], window)
        bias[c] = jnp.where(visible[:8] > 0.5, 0.0, NEG)

    def fill_bias_t(c):
        parts = []
        for s in range(3):
            from_slot = block_rows(nbuf[c + s, tokens:, PAIR : 2 * PAIR], tokens)
            parts.append(from_slot[(2 - s) * local : (3 - s) * local])
        visible = jnp.concatenate(parts, axis=1)
        bias_t[c, :local, :] = jnp.where(visible > 0.5, 0.0, NEG)

    head_group = head_row[0:1, pl.ds(pl.multiple_of(me.g * gw, gw), gw)]
    head_rows = jnp.broadcast_to(head_group, (16, gw)).astype(BF16)

    def forward(c):
        fill_bias(c)
        hide = bias[c]
        net = jnp.zeros((16, tokens), F32)
        found = jnp.zeros((tokens, PAIR), F32)
        for p in range(PAIRS):
            q_part = slice(p * TRIO, p * TRIO + PAIR)
            k_part = slice(p * TRIO + PAIR, p * TRIO + 2 * PAIR)
            v_part = slice(p * TRIO + 2 * PAIR, (p + 1) * TRIO)
            query = qbuf[c + 1, :, q_part] * jnp.asarray(SCALE, BF16)
            keys = qbuf[pl.ds(c, 3), :, k_part].reshape(window, PAIR)
            vals = qbuf[pl.ds(c, 3), :, v_part].reshape(window, PAIR)
            outs = []
            for half in range(2):
                mine = low if half == 0 else jnp.logical_not(low)
                scores = dot_nt(jnp.where(mine, query, jnp.zeros_like(query)), keys) + spread(hide, local)
                top = jnp.max(scores, axis=1, keepdims=True)
                expo = jnp.exp(scores - top)
                norm = jnp.sum(expo, axis=1, keepdims=True)
                probs_b = (expo * (1.0 / norm)).astype(BF16)
                outs.append(dot_nn(probs_b, vals))
                found = jnp.where(lane == 2 * p + half, top + jnp.log(norm), found)
            value = jnp.where(low, outs[0], outs[1]).astype(BF16)
            attn[c, :, p * PAIR : (p + 1) * PAIR] = value
            net = net + dot_nt(head_rows[:, p * PAIR : (p + 1) * PAIR], value)
        stats[c] = found
        mbuf[0, c] = net[:8]

    def inner_chunk(i, carry):
        forward(i)
        return carry

    lax.fori_loop(1, GROUP - 1, inner_chunk, 0)
    halo_copy().wait_recv()
    halo_forward(near_halo).start()
    project(near_halo)
    halo_forward(other_halo).wait_recv()
    project(other_halo)

    def outer_chunk(i, carry):
        forward(i * (GROUP - 1))
        return carry

    lax.fori_loop(0, 2, outer_chunk, 0)

    in_row = lax.broadcasted_iota(jnp.int32, (8, tokens), 0)
    for c in range(GROUP):
        mbuf[0, c] = jnp.where(in_row == 0, mbuf[0, c], 0.0)
    extra = jnp.where(
        in_row == 0, base_row + noise_ref[...], jnp.where(in_row == 1, 2.0 * (1.0 - small[1:2, :]), 0.0)
    )
    mbuf[0, me.g] = mbuf[0, me.g] + extra

    def net_copy(o):
        return remote(mbuf.at[0], mbuf.at[o], m_send.at[o - 1], m_recv.at[o - 1], g_peers[o - 1])

    for o in range(1, GROUP):
        net_copy(o).start()
    for c in range(GROUP):
        fill_bias_t(c)
    for o in range(1, GROUP):
        net_copy(o).wait_recv()

    def d_attn_parts(row):
        col = jnp.broadcast_to(row, (PAIR, tokens)).T
        return col, [(col * head_group[:, p * PAIR : (p + 1) * PAIR]).astype(BF16) for p in range(PAIRS)]

    def finish_stats(c):
        msg = mbuf[0, c] + mbuf[1, c] + mbuf[2, c] + mbuf[3, c]
        col, parts = d_attn_parts(msg[0:1] * msg[1:2])
        full = jnp.where(lane == 8, col, stats[c])
        for p, value in enumerate(parts):
            dattn[c + 1, :, p * PAIR : (p + 1) * PAIR] = value
            prod = value.astype(F32) * attn[c, :, p * PAIR : (p + 1) * PAIR].astype(F32)
            sum_low = jnp.sum(jnp.where(low, prod, 0.0), axis=1, keepdims=True)
            sum_high = jnp.sum(jnp.where(low, 0.0, prod), axis=1, keepdims=True)
            full = jnp.where(lane == 4 + 2 * p, sum_low, full)
            full = jnp.where(lane == 5 + 2 * p, sum_high, full)
        stats[c] = full
        rbuf[c + 1] = full.T[:16, :]

    up_copy = remote(rbuf.at[GROUP], rbuf.at[0], r_send.at[0], r_recv.at[0], me.at(z=up_z))
    down_copy = remote(rbuf.at[1], rbuf.at[SLOTS - 1], r_send.at[1], r_recv.at[1], me.at(z=down_z))
    finish_stats(0)
    down_copy.start()
    finish_stats(GROUP - 1)
    up_copy.start()
    for c in range(1, GROUP - 1):
        finish_stats(c)

    def backward(c, p):
        q_part = slice(p * TRIO, p * TRIO + PAIR)
        k_part = slice(p * TRIO + PAIR, p * TRIO + 2 * PAIR)
        v_part = slice(p * TRIO + 2 * PAIR, (p + 1) * TRIO)
        a_part = slice(p * PAIR, (p + 1) * PAIR)
        hide = bias[c]
        hide_t = bias_t[c]
        found = stats[c]
        scale = jnp.asarray(SCALE, BF16)
        query = qbuf[pl.ds(c, 3), :, q_part].reshape(window, PAIR) * scale
        own_query = qbuf[c + 1, :, q_part] * scale
        keys = qbuf[pl.ds(c, 3), :, k_part].reshape(window, PAIR)
        vals = qbuf[pl.ds(c, 3), :, v_part].reshape(window, PAIR)
        own_keys = qbuf[c + 1, :, k_part]
        own_vals = qbuf[c + 1, :, v_part]
        d_attn = dattn[pl.ds(c, 3), :, a_part].reshape(window, PAIR)
        own_d_attn = dattn[c + 1, :, a_part]
        rows_of = [rbuf[c + s] for s in range(3)]
        d_q, d_k, d_v = [], [], []
        for half in range(2):
            mine = low if half == 0 else jnp.logical_not(low)
            h = 2 * p + half
            lse = found[:, h : h + 1]
            delta = found[:, 4 + h : 5 + h]
            probs = jnp.exp(
                dot_nt(jnp.where(mine, own_query, jnp.zeros_like(own_query)), keys) + spread(hide, local) - lse
            )
            d_probs = dot_nt(jnp.where(mine, own_d_attn, jnp.zeros_like(own_d_attn)), vals)
            d_scores = (probs * (d_probs - delta)).astype(BF16)
            d_q.append(dot_nn(d_scores, keys))
            lse_row = jnp.concatenate([r[h : h + 1] for r in rows_of], axis=1)
            delta_row = jnp.concatenate([r[4 + h : 5 + h] for r in rows_of], axis=1)
            own_keys_m = jnp.where(mine, own_keys, jnp.zeros_like(own_keys))
            own_vals_m = jnp.where(mine, own_vals, jnp.zeros_like(own_vals))
            probs_t = jnp.exp(dot_nt(own_keys_m, query) + spread(hide_t, local) - lse_row)
            d_v.append(dot_nn(probs_t.astype(BF16), d_attn))
            d_probs_t = dot_nt(own_vals_m, d_attn)
            d_scores_t = (probs_t * (d_probs_t - delta_row)).astype(BF16)
            d_k.append(dot_nn(d_scores_t, query))
        at = pl.ds(pl.multiple_of(c * tokens, tokens), tokens) if not isinstance(c, int) else slice(
            c * tokens, (c + 1) * tokens
        )
        dqkv[at, p * TRIO : p * TRIO + PAIR] = (jnp.where(low, d_q[0], d_q[1]) * SCALE).astype(BF16)
        dqkv[at, p * TRIO + PAIR : p * TRIO + 2 * PAIR] = jnp.where(low, d_k[0], d_k[1]).astype(BF16)
        dqkv[at, p * TRIO + 2 * PAIR : (p + 1) * TRIO] = jnp.where(low, d_v[0], d_v[1]).astype(BF16)

    def y_copy(o, k):
        return remote(
            y_buf.at[o - 1, k], y_got.at[o - 1, k], y_send.at[o - 1, k], y_recv.at[o - 1, k], f_peers[o - 1]
        )

    def product(f, p):
        at = pl.ds(pl.multiple_of(f * rows, rows), rows)
        return dot_nn(nt[at, :], dqkv[:, p * TRIO : (p + 1) * TRIO])

    def pieces(p):
        for j in range(3):
            for r in range(SPLIT):
                yield (p * 3 + j) * SPLIT + r, slice(r * rc, (r + 1) * rc), slice(j * PAIR, (j + 1) * PAIR)

    def send_grads(p):
        for o in range(1, nf):
            part = product((me.f + o) % nf, p).astype(BF16)
            for k, r_at, c_at in pieces(p):
                y_buf[o - 1, k] = part[r_at, c_at]
                y_copy(o, k).start()

    def keep_grads(p):
        part = product(me.f, p)
        for k, r_at, c_at in pieces(p):
            acc[k] = part[r_at, c_at]

    lower = me.z < nz // 2
    depth = jnp.where(lower, me.z, nz - 1 - me.z)
    outer = depth == 0
    has_outer = jnp.logical_not(outer)
    inner = depth == nz // 2 - 1
    not_inner = jnp.logical_not(inner)
    inward = me.at(z=jnp.where(lower, up_z, down_z))
    outward = me.at(z=jnp.where(lower, down_z, up_z))

    def z_copy(k, way):
        return remote(z_buf.at[k], z_got.at[way, k], z_send.at[0, k], z_recv.at[way, k], inward)

    def result_copy(k):
        ref = res.at[me.g, k]
        return remote(ref, ref, z_send.at[1, k], z_recv.at[2, k], outward)

    def g_copy(g, k, way, to):
        return remote(res.at[g, k], res.at[g, k], g_send.at[way, k], g_recv.at[way, k], to)

    def place_result(g, k):
        p, j, r = k // per_pair, k // SPLIT % 3, k % SPLIT
        at = pl.ds(pl.multiple_of(j * width + g * gw + p * PAIR, PAIR), PAIR)
        grad_out[r * rc : (r + 1) * rc, at] = res[g, k].astype(F32)

    def stage_a(k):
        value = acc[k]
        for o in range(1, nf):
            y_copy(o, k).wait_recv()
            value = value + y_got[o - 1, k].astype(F32)
        acc[k] = value

        @pl.when(outer)
        def _():
            z_buf[k] = acc[k].astype(BF16)
            z_copy(k, 0).start()

    def stage_b(k):
        @pl.when(has_outer)
        def _():
            z_copy(k, 0).wait_recv()
            z_buf[k] = (acc[k] + z_got[0, k].astype(F32)).astype(BF16)

            @pl.when(inner)
            def _():
                z_copy(k, 1).start()

            @pl.when(not_inner)
            def _():
                z_copy(k, 0).start()

    def stage_c(k):
        @pl.when(inner)
        def _():
            z_copy(k, 1).wait_recv()
            res[me.g, k] = (z_buf[k].astype(F32) + z_got[1, k].astype(F32)).astype(BF16)

        @pl.when(not_inner)
        def _():
            result_copy(k).wait_recv()

        @pl.when(has_outer)
        def _():
            result_copy(k).start()

        g_copy(me.g, k, 0, to_x).start()
        g_copy(me.g, k, 1, to_core).start()
        place_result(me.g, k)

    def stage_d(k):
        g_copy(me.g_x, k, 0, to_x).wait_recv()
        g_copy(me.g_x, k, 2, to_core).start()
        place_result(me.g_x, k)

    def stage_e(k):
        g_copy(me.g_core, k, 1, to_core).wait_recv()
        place_result(me.g_core, k)
        g_copy(me.g_far, k, 2, to_core).wait_recv()
        place_result(me.g_far, k)

    def inner_backward(i, carry):
        backward(i, 0)
        return carry

    lax.fori_loop(1, GROUP - 1, inner_backward, 0)
    up_copy.wait_recv()
    down_copy.wait_recv()
    for j in (0, SLOTS - 1):
        unused, parts = d_attn_parts(rbuf[j][8:9, :])
        for p, value in enumerate(parts):
            dattn[j, :, p * PAIR : (p + 1) * PAIR] = value

    def outer_backward(i, carry):
        backward(i * (GROUP - 1), 0)
        return carry

    lax.fori_loop(0, 2, outer_backward, 0)
    send_grads(0)
    keep_grads(0)

    def d_normed(g):
        at = pl.ds(pl.multiple_of(g * tokens, tokens), tokens)
        return dot_nt(dqkv[at, :], wbuf[...])

    def d_copy(at):
        to = to_x if at == 2 else to_core
        return remote(dn_buf.at[at], dn_got.at[at], d_send.at[at], d_recv.at[at], to)

    def far_backward(i, carry):
        backward(jnp.where(i == 0, me.g_far, me.g_x), 1)
        return carry

    def near_backward(i, carry):
        backward(jnp.where(i == 0, me.g_core, me.g), 1)
        return carry

    lax.fori_loop(0, 2, far_backward, 0)
    dn_buf[0] = d_normed(me.g_far).astype(BF16)
    d_copy(0).start()
    dn_acc[...] = d_normed(me.g_x)
    d_copy(0).wait_recv()
    dn_buf[2] = (dn_acc[...] + dn_got[0].astype(F32)).astype(BF16)
    d_copy(2).start()
    stage_a(0)
    near_backward(0, 0)
    stage_a(1)
    near_backward(1, 0)
    send_grads(1)
    stage_b(0)
    dn_buf[1] = d_normed(me.g_core).astype(BF16)
    d_copy(1).start()
    keep_grads(1)
    dn_acc[...] = d_normed(me.g)
    for t in range(2, chunks + LAG_C):
        if t < chunks:
            stage_a(t)
        for k in range(chunks):
            if k and max(k + LAG_B, 2) == t:
                stage_b(k)
            if max(k + LAG_C, 2) == t:
                stage_c(k)

    d_copy(1).wait_recv()
    d_copy(2).wait_recv()

    def hidden_tile(i, carry):
        at = pl.ds(pl.multiple_of(i * step, step), step)
        d_norm = dn_acc[at, :] + dn_got[1, at, :].astype(F32) + dn_got[2, at, :].astype(F32)
        h_in = hbuf[at, :]
        inv = lax.rsqrt(jnp.mean(h_in * h_in, axis=1, keepdims=True) + EPS)
        d_out = stats[me.g, at, 8:9] * head
        mean = jnp.mean(d_norm * h_in, axis=1, keepdims=True)
        d_hidden_out[at, :] = (d_out + inv * (d_norm - h_in * inv * inv * mean)).astype(BF16)
        return carry

    lax.fori_loop(0, tokens // step, hidden_tile, 0)
    for k in range(chunks):
        stage_d(k)
        if k:
            stage_e(k - 1)
    stage_e(chunks - 1)

    for o in range(1, nf):
        for i in range(4):
            w_copy(i, o).wait_send()
        for i in range(2):
            w_pass_copy(i, o).wait_send()
    for part in range(2):
        for way, to in ((0, to_x), (1, to_core)):
            token_copy(slot, part, way, to).wait_send()
        token_copy(x_slot, part, 2, to_core).wait_send()
    halo_copy().wait_send()
    halo_forward(near_halo).wait_send()
    for o in range(1, GROUP):
        net_copy(o).wait_send()
    up_copy.wait_send()
    down_copy.wait_send()
    for at in range(3):
        d_copy(at).wait_send()
    for k in range(chunks):
        for o in range(1, nf):
            y_copy(o, k).wait_send()
        z_copy(k, 0).wait_send()
        g_copy(me.g, k, 0, to_x).wait_send()
        g_copy(me.g, k, 1, to_core).wait_send()
        g_copy(me.g_x, k, 2, to_core).wait_send()

    @pl.when(has_outer)
    def _():
        for k in range(chunks):
            result_copy(k).wait_send()


def layer_call(nf, nz, hidden, w, cvec, head, freq, time_idx, cond_mask, noise, blocks, counts):
    tokens, width = hidden.shape
    rows = width // nf
    rc = rows // SPLIT
    chunks = PAIRS * 3 * SPLIT
    gw = width // GROUP
    dma = pltpu.SemaphoreType.DMA
    return pl.pallas_call(
        functools.partial(layer_kernel, nf, nz),
        in_specs=[HBM] * 10,
        out_specs=[VMEM, VMEM],
        out_shape=[
            pltpu.VMEM((rows, 3 * width), F32),
            pltpu.VMEM((tokens, width), BF16),
        ],
        scratch_shapes=[
            pltpu.VMEM(hidden.shape, BF16),
            pltpu.VMEM(cvec.shape, BF16),
            pltpu.VMEM(head.shape, BF16),
            pltpu.VMEM(freq.shape, F32),
            pltpu.VMEM(time_idx.shape, jnp.int32),
            pltpu.VMEM(cond_mask.shape, jnp.int32),
            pltpu.VMEM(noise.shape, F32),
            pltpu.SMEM(blocks.shape, jnp.int32),
            pltpu.SMEM(counts.shape, jnp.int32),
            pltpu.VMEM((1, width), F32),
            pltpu.VMEM((SLOTS, tokens + 16, width), BF16),
            pltpu.VMEM((width, GROUP * tokens), BF16),
            pltpu.VMEM((width, 3 * gw), BF16),
            pltpu.VMEM((tokens, width), F32),
            pltpu.VMEM((SLOTS, tokens, 3 * gw), BF16),
            pltpu.VMEM((tokens, PAIR), F32),
            pltpu.VMEM((tokens, PAIR), F32),
            pltpu.VMEM((GROUP, 8, 3 * tokens), F32),
            pltpu.VMEM((GROUP, 8, 3 * tokens), F32),
            pltpu.VMEM((GROUP, tokens, gw), BF16),
            pltpu.VMEM((GROUP, tokens, PAIR), F32),
            pltpu.VMEM((GROUP, GROUP, 8, tokens), F32),
            pltpu.VMEM((SLOTS, 16, tokens), F32),
            pltpu.VMEM((SLOTS, tokens, gw), BF16),
            pltpu.VMEM((GROUP * tokens, 3 * gw), BF16),
            pltpu.VMEM((chunks, rc, PAIR), F32),
            pltpu.VMEM((nf - 1, chunks, rc, PAIR), BF16),
            pltpu.VMEM((nf - 1, chunks, rc, PAIR), BF16),
            pltpu.VMEM((chunks, rc, PAIR), BF16),
            pltpu.VMEM((2, chunks, rc, PAIR), BF16),
            pltpu.VMEM((GROUP, chunks, rc, PAIR), BF16),
            pltpu.VMEM((tokens, width), F32),
            pltpu.VMEM((3, tokens, width), BF16),
            pltpu.VMEM((3, tokens, width), BF16),
            dma((nf - 1, 3 * PAIRS)),
            dma((nf - 1, 3 * PAIRS)),
            dma((3 * PAIRS,)),
            dma((3, 2)),
            dma((3, 2)),
            dma((2,)),
            dma((2,)),
            dma((GROUP - 1,)),
            dma((GROUP - 1,)),
            dma((2,)),
            dma((2,)),
            dma((nf - 1, chunks)),
            dma((nf - 1, chunks)),
            dma((2, chunks)),
            dma((3, chunks)),
            dma((3, chunks)),
            dma((3, chunks)),
            dma((3,)),
            dma((3,)),
            dma((9,)),
        ],
        compiler_params=pltpu.CompilerParams(
            collective_id=0, has_side_effects=True, vmem_limit_bytes=54 << 20
        ),
        name="layer",
    )(hidden, w, cvec, head, freq, time_idx, cond_mask, noise, blocks, counts)


def body(hidden, w_qkv, cond_vec, head_w, blocks, counts, time_idx, cond_mask, noise):
    width = hidden.shape[2]
    half = width // 2
    nf = lax.axis_size("fsdp")
    nz = lax.axis_size("seq") // GROUP
    freq = np.exp(np.float32(-math.log(10000.0)) * np.arange(half, dtype=np.float32) / np.float32(half))
    grad, d_hidden = layer_call(
        nf,
        nz,
        hidden[0],
        w_qkv,
        cond_vec.reshape(width // PAIR, PAIR),
        head_w.reshape(width // PAIR, PAIR),
        jnp.asarray(freq.astype(np.float32))[None, :],
        time_idx,
        cond_mask,
        noise,
        blocks,
        counts,
    )
    return (d_hidden[None], grad)


def solution(mesh):
    return jax.shard_map(
        body,
        mesh=mesh,
        in_specs=(
            P("fsdp", "seq", None),
            P("fsdp", None),
            P(),
            P(),
            P("fsdp", "seq", None),
            P("fsdp", "seq"),
            P("fsdp", "seq"),
            P("fsdp", "seq"),
            P("fsdp", "seq"),
        ),
        out_specs=(P("fsdp", "seq", None), P("fsdp", None)),
        check_vma=False,
    )
```
